32 devices in a mesh: dp: 2 (over x), slab: 16 (over z, y, core).
Axes of the slice: x: 2, y: 2, z: 4, core: 2. Of those that a mesh axis runs over, the one named last changes fastest.
Arguments:
- images: float32 [512, 128, 128], P(('dp', 'slab')), may hold values from -6 to 6
- defocus: float32 [512], P(('dp', 'slab')), may hold values from 8 to 40
- references: float32 [512, 64, 128], P('slab'), may hold values from -6 to 6
- orient_owner: int32 [512, 4], P(('dp', 'slab')), may hold values from 0 to 15, all different within a row; in each aligned block of 16 rows (0 to 15, 16 to 31, ...) at most 8 rows name the same one
- orient_local: int32 [512, 4], P(('dp', 'slab')), may hold values from 0 to 31
- block_owner: int32 [512, 8, 1], P('slab'), may hold values from 0 to 15; in each aligned block of 256 rows (0 to 255, 256 to 511, ..., all dimensions but the last counted through in order) at most 32 rows name the same one
- block_cell: int32 [512, 8], P('slab'), may hold values from 0 to 511
Outputs:
- posterior: float32 [512, 4], P(('dp', 'slab'))
- volume: float32 [64, 256, 2, 256], P('slab', 'dp')
The draws below stay inside these ranges and needn't reach their ends.
Inputs may be any that keep to these rules, and one draw needn't show every extreme that they name: `orient_owner`: within the 16 particles of one device (aligned blocks of rows), no slab index is named by more than 8 entries, and some slab index is named by exactly 8; the 4 entries of a particle differ. `block_owner`: within the 256 blocks of one slab index's references (aligned blocks of rows), no slab index is named by more than 32 entries, and some slab index is named by exactly 32.
All inputs are finite; a program needn't handle non-finite values.
Results may differ from the reference program's by a relative error of at most 0.00015.
Values sent between devices are 32-bit elements; how exact they have to be, the bound alone decides.
A program may use at most 64 MiB of HBM per device.

```python
import math
import jax
import jax.numpy as jnp
import numpy as np
from jax import lax

IMG = 128
FB = 64
VY = 256
VX = 256
BAND = 8
K = 4
P_DEV = 16
REF_DEV = 32
OWNERS = 16
PARTICLES = 512
REFS = 512
NZ = 64
BANDS = 8
CELLS = 512
PCAP = 8
BCAP = 32
N_SLAB = 16


def plant(array, rng, smallest, high):
    longest = array.shape.index(max(array.shape))
    spots = []
    for shift in (0, 1):
        where = [jax.random.randint(jax.random.fold_in(rng, axis), (), 0, length) for axis, length in enumerate(array.shape)]
        where[longest] = (where[longest] + shift) % array.shape[longest]
        spots.append(tuple(where))
    return array.at[spots[0]].set(smallest).at[spots[1]].set(high)


def level_of(own_key, dims, split, smallest, largest):
    def one(position, parts):
        steps = jax.random.uniform(jax.random.fold_in(jax.random.fold_in(own_key, 6), position), (parts,), jnp.float32, smallest / len(split), largest / len(split))
        return jnp.repeat(jnp.exp(steps), dims[position] // parts).reshape((-1,) + (1,) * (len(dims) - position - 1))

    loudness = one(*split[0])
    for cut in split[1:]:
        loudness = loudness * one(*cut)
    return loudness


def shared_out(rng, own, number, rows, count, top, most, lean):
    ranking = jax.random.permutation(rng, count)
    packed, ordinary = shares(count, rows * top, most, lean, True), shares(count, rows * top, most, lean, False)
    places = jnp.arange(count)

    def named(lengths, turn):
        used = int((lengths > 0).sum())
        fixed = max(1, used // 4)
        shifted = fixed + (places - fixed + turn * (used - fixed)) % max(1, count - fixed)
        return jnp.zeros((count,), jnp.int32).at[ranking[jnp.where(places < fixed, places, shifted)]].set(jnp.asarray(lengths, jnp.int32))

    lengths = jnp.where(number % 4 == 0, named(packed, number // 4), named(ordinary, number - number // 4 - 1))
    mixed = jax.random.permutation(jax.random.fold_in(own, 3), count)
    source_of, sink = mixed[0:count // 2 * 2:2], mixed[1:count // 2 * 2:2]
    slack = jnp.minimum(lengths[source_of] - 1, most - lengths[sink]) // 2
    slack = jnp.where((source_of == ranking[0]) | (sink == ranking[0]) | (lengths[sink] == 0), 0, jnp.maximum(slack, 0))
    shifted = jax.random.randint(jax.random.fold_in(own, 4), (count // 2,), 0, 1 << 20) % (slack + 1)
    lengths = lengths.at[source_of].add(-shifted).at[sink].add(shifted)
    members = jnp.searchsorted(jnp.cumsum(lengths), jnp.arange(rows * top), side="right").astype(jnp.int32)
    listing = members.reshape(top, rows).T
    listing = listing[jax.random.permutation(jax.random.fold_in(own, 1), rows)]
    turn = jax.random.randint(jax.random.fold_in(own, 2), (rows, 1), 0, top)
    return jnp.take_along_axis(listing, (jnp.arange(top)[None, :] + turn) % top, axis=1)


def shares(number_of, total, reach, skew, full):
    loads = [(1 << 20) // math.isqrt(standing ** skew) + 1 for standing in range(1, number_of + 1)]
    largest = reach if full else min(reach, max(-(-total // number_of), total * loads[0] // sum(loads)))
    least = 1 if total - largest >= number_of - 1 else 0
    given, surplus = [largest] + [least] * (number_of - 1), total - largest - least * (number_of - 1)
    while surplus > 0:
        movable = [i for i in range(1, number_of) if given[i] < largest] or [i for i in range(1, number_of) if given[i] < reach]
        mass, remaining = sum([loads[i] for i in movable]), surplus
        for i in movable:
            addition = min(reach - given[i], max(1, remaining * loads[i] // mass), surplus)
            given[i] = given[i] + addition
            surplus = surplus - addition
    return np.array(given)


def scatter_about(rng, shape, width, reach, shards=(), kind=jnp.bfloat16):
    level = level_of(rng, shape, shards, -0.22, 0.18) if shards else 1.0
    values = jax.random.normal(rng, shape, jnp.float32) * width * level
    return jnp.minimum(jnp.maximum(values, -reach), reach).astype(kind)


def setup_inputs(seed: int = 0) -> dict:
    arg_keys = jax.random.split(jax.random.key(seed), 8)
    images = scatter_about(arg_keys[0], (PARTICLES, IMG, IMG), 1.0, 6.0, ((0, 32),), jnp.float32)
    defocus = jnp.clip(jnp.exp(math.log(40.0) - 1.609438 * jax.random.uniform(arg_keys[1], (PARTICLES,), jnp.float32) ** level_of(arg_keys[1], (PARTICLES,), ((0, 32),), -0.2, 0.2)), 8.0, 40.0)
    references = scatter_about(arg_keys[2], (REFS, FB, 2 * FB), 1.0, 6.0, ((0, 16),), jnp.float32)
    orient_owner_keys = jax.random.split(jax.random.fold_in(arg_keys[3], 1), PARTICLES // P_DEV)
    orient_owner_turns = jax.random.permutation(jax.random.fold_in(arg_keys[3], 3), PARTICLES // P_DEV)
    orient_owner = jax.vmap(lambda own, number: shared_out(jax.random.fold_in(arg_keys[3], 2), own, number, P_DEV, OWNERS, K, PCAP, 2))(orient_owner_keys, orient_owner_turns).reshape((PARTICLES, K))
    orient_local = plant(jax.random.randint(arg_keys[4], (PARTICLES, K), 0, REF_DEV), jax.random.fold_in(arg_keys[4], 1), 0, REF_DEV - 1).astype(jnp.int32)
    block_owner_keys = jax.random.split(jax.random.fold_in(arg_keys[5], 1), REFS * BANDS // (REF_DEV * BANDS))
    block_owner_turns = jax.random.permutation(jax.random.fold_in(arg_keys[5], 3), REFS * BANDS // (REF_DEV * BANDS))
    block_owner = jax.vmap(lambda own, number: shared_out(jax.random.fold_in(arg_keys[5], 2), own, number, REF_DEV * BANDS, OWNERS, 1, BCAP, 2))(block_owner_keys, block_owner_turns).reshape((REFS, BANDS, 1))
    block_cell = plant(jax.random.randint(arg_keys[6], (REFS, BANDS), 0, CELLS), jax.random.fold_in(arg_keys[6], 1), 0, CELLS - 1).astype(jnp.int32)
    return dict(images=images, defocus=defocus, references=references, orient_owner=orient_owner, orient_local=orient_local, block_owner=block_owner, block_cell=block_cell)


AMPLITUDE = 0.1
EPSILON = 1e-05

def contrast(defocus, frequency_total):
    freqs = (jnp.arange(frequency_total, dtype=jnp.int32) - frequency_total // 2).astype(jnp.float32)
    radius = (freqs[:, None] * freqs[:, None] + freqs[None, :] * freqs[None, :]) / float((frequency_total // 2) ** 2)
    phase = defocus[:, None, None] * radius[None]
    return -(math.sqrt(1.0 - AMPLITUDE * AMPLITUDE) * jnp.sin(phase) + AMPLITUDE * jnp.cos(phase))

def reference(images, defocus, references, orient_owner, orient_local, block_owner, block_cell):
    freq_index = jnp.mod(jnp.arange(FB, dtype=jnp.int32) - FB // 2, IMG).astype(jnp.int32)
    weights = contrast(defocus, FB) / IMG

    def spectrum(couple):
        image, factor = couple
        full_map = jnp.fft.fft2(image)
        cropped = full_map[freq_index][:, freq_index]
        return jnp.concatenate([jnp.real(cropped) * factor, jnp.imag(cropped) * factor], axis=1)
    spectra = lax.map(spectrum, (images, weights))
    ref_ids = (orient_owner * REF_DEV + orient_local).astype(jnp.int32)

    def scores_of(couple):
        spec, ids = couple
        chosen = references[ids]
        ref_re, ref_im = (chosen[..., :FB], chosen[..., FB:])
        spec_re, spec_im = (spec[None, :, :FB], spec[None, :, FB:])
        prod_re = ref_re * spec_re + ref_im * spec_im
        prod_im = ref_re * spec_im - ref_im * spec_re
        embed_re = jnp.zeros((ids.shape[0], IMG, IMG), jnp.float32).at[:, freq_index[:, None], freq_index[None, :]].set(prod_re)
        embed_im = jnp.zeros((ids.shape[0], IMG, IMG), jnp.float32).at[:, freq_index[:, None], freq_index[None, :]].set(prod_im)
        translation_offsets = jnp.real(jnp.fft.ifft2(lax.complex(embed_re, embed_im))) * (IMG * IMG / FB)
        return lax.optimization_barrier(jnp.max((translation_offsets * translation_offsets).reshape(ids.shape[0], -1), axis=1)) + EPSILON
    scores = lax.map(scores_of, (spectra, ref_ids))
    posterior = scores / lax.optimization_barrier(jnp.sum(scores, axis=1, keepdims=True))
    averages = jnp.zeros((REFS, FB, 2 * FB), jnp.float32)
    for column in range(K):
        averages = averages + jax.ops.segment_sum(posterior[:, column, None, None] * spectra, ref_ids[:, column], num_segments=REFS)
    pieces = averages.reshape(REFS * BANDS, BAND, 2 * FB)
    target = (block_owner.reshape(-1) * CELLS + block_cell.reshape(-1)).astype(jnp.int32)
    summed = jax.ops.segment_sum(pieces, target, num_segments=N_SLAB * CELLS)
    row_blocks = VY // BAND
    col_blocks = VX // FB
    volume = summed.reshape(NZ, row_blocks, col_blocks, BAND, 2, FB).transpose(0, 1, 3, 4, 2, 5).reshape(NZ, VY, 2, VX)
    return (posterior, volume)
```

```python
import functools
import math

import jax
import jax.numpy as jnp
import numpy as np
from jax import lax
from jax.experimental import pallas as pl
from jax.experimental.pallas import tpu as pltpu
from jax.sharding import PartitionSpec as P

VY = 256
VX = 256
ZDEV = 4


HIGH_PRECISION = lax.Precision.HIGHEST
AMPLITUDE = 0.1
EPSILON = 1e-05


def freq_tables(image_side, frequency_total):
    pixels = jnp.arange(image_side, dtype=jnp.int32)
    freqs = jnp.arange(frequency_total, dtype=jnp.int32) - frequency_total // 2
    phase = jnp.mod(pixels[:, None] * freqs[None, :], image_side).astype(jnp.float32) * (
        2.0 * math.pi / image_side
    )
    return (jnp.cos(phase), jnp.sin(phase))


def contrast(defocus, frequency_total):
    freqs = (jnp.arange(frequency_total, dtype=jnp.int32) - frequency_total // 2).astype(
        jnp.float32
    )
    radius = (freqs[:, None] * freqs[:, None] + freqs[None, :] * freqs[None, :]) / float(
        (frequency_total // 2) ** 2
    )
    phase = defocus[:, None, None] * radius[None]
    return -(math.sqrt(1.0 - AMPLITUDE * AMPLITUDE) * jnp.sin(phase) + AMPLITUDE * jnp.cos(phase))


def spectra_of(images, defocus, frequency_total):
    image_side = images.shape[-1]
    cosine, sine = freq_tables(image_side, frequency_total)
    first_pass = jnp.einsum(
        "pyx,xf->pyf", images, jnp.concatenate([cosine, -sine], axis=1), precision=HIGH_PRECISION
    )
    lower_half = jnp.concatenate(
        [first_pass[..., frequency_total:], -first_pass[..., :frequency_total]], axis=2
    )
    spectra = jnp.einsum("yf,pyg->pfg", cosine, first_pass, precision=HIGH_PRECISION) + jnp.einsum(
        "yf,pyg->pfg", sine, lower_half, precision=HIGH_PRECISION
    )
    factor = contrast(defocus, frequency_total) / image_side
    return spectra * jnp.concatenate([factor, factor], axis=2)


def score_slots(chosen, received, image_side):
    frequency_total = received.shape[1]
    cosine, sine = freq_tables(image_side, frequency_total)
    rotation_angle = jnp.concatenate(
        [jnp.concatenate([cosine.T, sine.T], axis=1), jnp.concatenate([-sine.T, cosine.T], axis=1)],
        axis=0,
    )
    inverted_rows = jnp.concatenate([cosine, -sine], axis=1)
    slot_total = received.shape[0]
    group_size = math.gcd(slot_total, 16)

    def one_group(couple):
        ref_part, spec_part = couple
        ref_re, ref_im = (ref_part[..., :frequency_total], ref_part[..., frequency_total:])
        spec_re, spec_im = (spec_part[..., :frequency_total], spec_part[..., frequency_total:])
        spectral_product = jnp.concatenate(
            [ref_re * spec_re + ref_im * spec_im, ref_re * spec_im - ref_im * spec_re], axis=2
        )
        center_index = jnp.einsum(
            "eio,ol->eil", spectral_product, rotation_angle, precision=HIGH_PRECISION
        )
        stacked_planes = jnp.concatenate(
            [center_index[..., :image_side], center_index[..., image_side:]], axis=1
        )
        translation_offsets = (
            jnp.einsum("kz,wzq->wkq", inverted_rows, stacked_planes, precision=HIGH_PRECISION)
            / frequency_total
        )
        return (
            jnp.max(
                (translation_offsets * translation_offsets).reshape(
                    translation_offsets.shape[0], -1
                ),
                axis=1,
            )
            + EPSILON
        )

    grouped = (
        chosen.reshape((slot_total // group_size, group_size) + chosen.shape[1:]),
        received.reshape((slot_total // group_size, group_size) + received.shape[1:]),
    )
    return lax.map(one_group, grouped).reshape(-1)


def slot_ranks(owner_ids, owner_count):
    owner_hits = (owner_ids[:, None] == jnp.arange(owner_count, dtype=jnp.int32)[None, :]).astype(
        jnp.int32
    )
    return jnp.sum((jnp.cumsum(owner_hits, axis=0) - 1) * owner_hits, axis=1)


def insert(blocks, cell_ids, planes, row_blocks, col_blocks, first_block, span_blocks):
    band_rows, row_width = (blocks.shape[2], blocks.shape[3])
    frequency_total = row_width // 2
    flat_rows = blocks.reshape(-1, band_rows * row_width)
    cell_ids = cell_ids.reshape(-1)
    plane_of = cell_ids // (row_blocks * col_blocks)
    row_of = cell_ids // col_blocks % row_blocks - first_block
    column_of = cell_ids % col_blocks
    usable = (cell_ids >= 0) & (row_of >= 0) & (row_of < span_blocks)
    target = jnp.where(usable, (plane_of * span_blocks + row_of) * col_blocks + column_of, -1)
    placing = (
        jnp.arange(planes * span_blocks * col_blocks, dtype=jnp.int32)[:, None] == target[None, :]
    ).astype(jnp.float32)
    placed = jnp.dot(placing, flat_rows, precision=HIGH_PRECISION)
    placed = placed.reshape(planes, span_blocks, col_blocks, band_rows, 2, frequency_total)
    return placed.transpose(0, 1, 3, 4, 2, 5).reshape(
        planes, span_blocks * band_rows, 2, col_blocks * frequency_total
    )


def per_device(images, defocus, references, orient_owner, orient_local, block_owner, block_cell):
    owner_count = lax.axis_size("slab")
    frequency_total = references.shape[1]
    image_side = images.shape[-1]
    part_count, pick_count = orient_owner.shape
    ref_rows = references.shape[0]
    slot_cap = max(2, 2 * part_count * pick_count // owner_count)
    spectra = spectra_of(images, defocus, frequency_total)
    flat_owner = orient_owner.reshape(-1)
    slot_of = flat_owner * slot_cap + slot_ranks(flat_owner, owner_count)
    particle_of = jnp.arange(part_count * pick_count, dtype=jnp.int32) // pick_count
    send_spectra = jnp.zeros(
        (owner_count * slot_cap, frequency_total, 2 * frequency_total), jnp.float32
    )
    send_spectra = send_spectra.at[slot_of].set(jnp.repeat(spectra, pick_count, axis=0))
    send_meta = jnp.full((owner_count * slot_cap, 2), -1, jnp.int32)
    send_meta = send_meta.at[slot_of].set(
        jnp.stack([orient_local.reshape(-1), particle_of], axis=1)
    )
    received, meta_in = (
        lax.all_to_all(
            send_spectra.reshape(owner_count, slot_cap, frequency_total, 2 * frequency_total),
            "slab",
            split_axis=0,
            concat_axis=0,
            tiled=True,
        ),
        lax.all_to_all(
            send_meta.reshape(owner_count, slot_cap, 2),
            "slab",
            split_axis=0,
            concat_axis=0,
            tiled=True,
        ),
    )
    flat_received = received.reshape(-1, frequency_total, 2 * frequency_total)
    ref_index = meta_in[..., 0].reshape(-1)
    chosen = references[jnp.clip(ref_index, 0, ref_rows - 1)]
    scores = score_slots(chosen, flat_received, image_side)
    slot_scores = scores.reshape(owner_count, slot_cap)
    back_scores = lax.all_to_all(slot_scores, "slab", split_axis=0, concat_axis=0, tiled=True)
    item_scores = back_scores.reshape(-1)[slot_of].reshape(part_count, pick_count)
    posterior = item_scores / jnp.sum(item_scores, axis=1, keepdims=True)
    slot_weight = (
        jnp.zeros((owner_count * slot_cap,), jnp.float32).at[slot_of].set(posterior.reshape(-1))
    )
    got_weight = lax.all_to_all(
        slot_weight.reshape(owner_count, slot_cap), "slab", split_axis=0, concat_axis=0, tiled=True
    ).reshape(-1)
    ref_hits = (ref_index[None, :] == jnp.arange(ref_rows, dtype=jnp.int32)[:, None]).astype(
        jnp.float32
    ) * got_weight[None, :]
    averages = jnp.dot(
        ref_hits, flat_received.reshape(flat_received.shape[0], -1), precision=HIGH_PRECISION
    )
    averages = averages.reshape(ref_rows, frequency_total, 2 * frequency_total)
    bands = block_cell.shape[1]
    band_rows = frequency_total // bands
    block_cap = max(2, 2 * ref_rows * bands // owner_count)
    dest_owner = block_owner.reshape(-1)
    block_slot = dest_owner * block_cap + slot_ranks(dest_owner, owner_count)
    cell_send = (
        jnp.full((owner_count * block_cap,), -1, jnp.int32)
        .at[block_slot]
        .set(block_cell.reshape(-1))
    )
    row_blocks = VY // band_rows
    col_blocks = VX // frequency_total
    pieces = averages.reshape(ref_rows * bands, band_rows, 2 * frequency_total)
    block_send = (
        jnp.zeros((owner_count * block_cap, band_rows, 2 * frequency_total), jnp.float32)
        .at[block_slot]
        .set(pieces)
    )
    blocks_in = lax.all_to_all(
        block_send.reshape(owner_count, block_cap, band_rows, 2 * frequency_total),
        "slab",
        split_axis=0,
        concat_axis=0,
        tiled=True,
    )
    cells_in = lax.all_to_all(
        cell_send.reshape(owner_count, block_cap), "slab", split_axis=0, concat_axis=0, tiled=True
    )
    partial_value = insert(blocks_in, cells_in, ZDEV, row_blocks, col_blocks, 0, row_blocks)
    volume = lax.psum_scatter(partial_value, "dp", scatter_dimension=1, tiled=True)
    return (posterior, volume)


HALF_PRECISION = lax.Precision.HIGH
MESH = pl.DeviceIdType.MESH


def ring_place(pos, depth):
    back = pos // depth
    z = (1 - back) * pos + back * (2 * depth - 1 - pos)
    return z * 2 + back


def gather_kernel(chips, own_ref, out_ref, local_sem, ring_send, ring_recv, pair_send, pair_recv):
    depth = chips // 2
    me = lax.axis_index("slab")
    core = me % 2
    chip = me // 2
    z, back = chip // 2, chip % 2
    pos = z + back * (2 * depth - 1 - 2 * z)
    dirs = ((pos + 1) % chips, (pos + chips - 1) % chips)
    targets = [ring_place(q, depth) * 2 + core for q in dirs]
    sibling = chip * 2 + 1 - core
    barrier = pltpu.get_barrier_semaphore()
    for other in targets + [sibling]:
        pl.semaphore_signal(barrier, inc=1, device_id={"slab": other}, device_id_type=MESH)
    pl.semaphore_wait(barrier, 3)
    part = own_ref.shape[0] // 2
    rows = lambda ref, h: ref.at[pl.ds(h * part, part)]
    local = pltpu.make_async_copy(own_ref, out_ref.at[me], local_sem)
    local.start()
    waits = []

    def ring_copy(src, origin, d, t, h):
        return pltpu.make_async_remote_copy(
            src_ref=src, dst_ref=rows(out_ref.at[origin], h),
            send_sem=ring_send.at[d, t, h], recv_sem=ring_recv.at[d, t, h],
            device_id={"slab": targets[d]}, device_id_type=MESH)

    def pair_copy(src, origin, n, h):
        return pltpu.make_async_remote_copy(
            src_ref=src, dst_ref=rows(out_ref.at[origin], h),
            send_sem=pair_send.at[n, h], recv_sem=pair_recv.at[n, h],
            device_id={"slab": sibling}, device_id_type=MESH)

    def origin_of(d, t):
        q = (pos + chips - t) % chips if d == 0 else (pos + t) % chips
        return ring_place(q, depth) * 2 + core

    hops = [(d, t, h) for t in range(depth) for h in range(2) for d in range(2)
            if t < depth - 1 or h == d]
    pair_of = lambda d, t, h: (t + 1 if d == 0 else depth + t + 1) if t < depth - 1 else depth
    for d, t, h in hops:
        if t == 0:
            copy = ring_copy(rows(own_ref, h), me, d, 0, h)
            copy.start()
            waits.append(copy)
    for h in range(2):
        copy = pair_copy(rows(own_ref, h), me, 0, h)
        copy.start()
        waits.append(copy)
    pairs = []
    for d, t, h in hops:
        origin = origin_of(d, t + 1)
        landed = rows(out_ref.at[origin], h)
        ring_copy(landed, origin, d, t, h).wait_recv()
        if (d, t + 1, h) in hops:
            copy = ring_copy(landed, origin, d, t + 1, h)
            copy.start()
            waits.append(copy)
        copy = pair_copy(landed, origin, pair_of(d, t, h), h)
        copy.start()
        pairs.append(copy)
        waits.append(copy)
    for copy in waits:
        copy.wait_send()
    pair_copy(rows(own_ref, 0), me, 0, 0).wait_recv()
    pair_copy(rows(own_ref, 1), me, 0, 1).wait_recv()
    for copy in pairs:
        copy.wait_recv()
    local.wait()


def ring_gather(payload, owner_count):
    chips = owner_count // 2
    depth = chips // 2
    return pl.pallas_call(
        functools.partial(gather_kernel, chips),
        out_shape=jax.ShapeDtypeStruct((owner_count,) + payload.shape, payload.dtype),
        in_specs=[pl.BlockSpec(memory_space=pl.ANY)],
        out_specs=pl.BlockSpec(memory_space=pl.ANY),
        scratch_shapes=[
            pltpu.SemaphoreType.DMA,
            pltpu.SemaphoreType.DMA((2, depth, 2)),
            pltpu.SemaphoreType.DMA((2, depth, 2)),
            pltpu.SemaphoreType.DMA((chips, 2)),
            pltpu.SemaphoreType.DMA((chips, 2)),
        ],
        compiler_params=pltpu.CompilerParams(collective_id=1, has_side_effects=True),
        name="ring_gather",
    )(payload)


def share_kernel(count, own_ref, out_ref, local_sem, send_sem, recv_sem):
    me = lax.axis_index("slab")
    barrier = pltpu.get_barrier_semaphore()
    others = [(me + step) % count for step in range(1, count)]
    for other in others:
        pl.semaphore_signal(barrier, inc=1, device_id={"slab": other}, device_id_type=MESH)
    local = pltpu.make_async_copy(own_ref, out_ref.at[me], local_sem)
    local.start()
    pl.semaphore_wait(barrier, count - 1)
    copies = []
    for n, other in enumerate(others):
        copy = pltpu.make_async_remote_copy(
            src_ref=own_ref, dst_ref=out_ref.at[me], send_sem=send_sem.at[n],
            recv_sem=recv_sem.at[n], device_id={"slab": other}, device_id_type=MESH)
        copy.start()
        copies.append(copy)
    for n, copy in enumerate(copies):
        copy.wait_send()
        source = (me + count - 1 - n) % count
        pltpu.make_async_remote_copy(
            src_ref=own_ref, dst_ref=out_ref.at[source], send_sem=send_sem.at[n],
            recv_sem=recv_sem.at[n], device_id={"slab": source}, device_id_type=MESH).wait_recv()
    local.wait()


def share(row, count):
    return pl.pallas_call(
        functools.partial(share_kernel, count),
        out_shape=jax.ShapeDtypeStruct((count,) + row.shape, row.dtype),
        in_specs=[pl.BlockSpec(memory_space=pltpu.VMEM)],
        out_specs=pl.BlockSpec(memory_space=pltpu.VMEM),
        scratch_shapes=[
            pltpu.SemaphoreType.DMA,
            pltpu.SemaphoreType.DMA((count - 1,)),
            pltpu.SemaphoreType.DMA((count - 1,)),
        ],
        compiler_params=pltpu.CompilerParams(collective_id=2, has_side_effects=True),
        name="share_scores",
    )(row)


GROUP = 8


def score_kernel(pidx, ridx, half_ref, a_ref, b_ref, whi_ref, wlo_ref, cc_ref, pat_ref, out_ref):
    step = pl.program_id(0)
    lines = half_ref.shape[1]
    f32, bf16 = jnp.float32, jnp.bfloat16
    products = []
    for e in range(GROUP):
        spec = half_ref[pidx[step * GROUP + e]]
        ref = ridx[step * GROUP + e]
        products.append(a_ref[ref] * spec + b_ref[ref] * pltpu.roll(spec, 64, 1))
    product = jnp.concatenate(products, axis=0)
    hi = product.astype(bf16)
    lo = (product - hi.astype(f32)).astype(bf16)
    dot = lambda x, y: jnp.dot(x, y, preferred_element_type=f32)
    turned = dot(hi, whi_ref[...]) + dot(lo, whi_ref[...]) + dot(hi, wlo_ref[...])
    edge = jnp.concatenate([p[33:34] for p in products], axis=0).T
    cosine, sine = pat_ref[0:1], pat_ref[1:2]
    stacks = []
    for e in range(GROUP):
        rows = turned[e * lines:(e + 1) * lines]
        er, ei = edge[0:lines, e:e + 1], edge[64:64 + lines, e:e + 1]
        both = jnp.concatenate(
            [rows[:, :128] + er * cosine - ei * sine, rows[:, 128:] + er * sine + ei * cosine], axis=0)
        high = both.astype(bf16)
        low = (both - high.astype(f32)).astype(bf16)
        stacks.append(jnp.concatenate([high, low, high], axis=0))
    peaks = []
    for e in range(0, GROUP, 2):
        shifts = jnp.abs(dot(cc_ref[...], jnp.concatenate(stacks[e:e + 2], axis=1)))
        best = jnp.max(shifts, axis=0, keepdims=True)
        peaks += [best[:, :128], best[:, 128:]]
    peak = jnp.max(jnp.concatenate(peaks, axis=0), axis=1, keepdims=True)
    out_ref[...] = jnp.broadcast_to(peak, (GROUP, 128))


def score_tables(image_side, frequency_total, lines):
    half = frequency_total // 2
    x = np.arange(image_side)
    freqs = np.arange(frequency_total) - half
    ang = 2 * np.pi * ((freqs[:, None] * x[None, :]) % image_side) / image_side
    cos, sin = np.cos(ang), np.sin(ang)
    w = np.block([[cos, sin], [-sin, cos]]) / frequency_total
    cr, sr = np.zeros((image_side, lines)), np.zeros((image_side, lines))
    cr[:, : half + 1], sr[:, : half + 1] = cos[: half + 1].T, sin[: half + 1].T
    c = np.concatenate([cr, -sr], axis=1)
    def two(m):
        high = m.astype(jnp.bfloat16)
        return high, (m - high.astype(np.float64)).astype(jnp.bfloat16)
    whi, wlo = two(w)
    chi, clo = two(c)
    pat = np.zeros((8, image_side), np.float32)
    pat[0] = np.array([1, 0, -1, 0])[x % 4] / frequency_total
    pat[1] = np.array([0, 1, 0, -1])[x % 4] / frequency_total
    return whi, wlo, np.concatenate([chi, chi, clo], axis=1), pat


def score_items(pidx, ridx, spectra, ref_a, ref_b, image_side, frequency_total):
    slots = pidx.shape[0]
    lines = spectra.shape[1]
    whi, wlo, cc, pat = (jnp.asarray(t) for t in score_tables(image_side, frequency_total, lines))
    full = lambda arr: pl.BlockSpec(arr.shape, lambda i, *_: (0,) * arr.ndim, pipeline_mode=pl.Buffered(1))
    args = (spectra, ref_a, ref_b, whi, wlo, cc, pat)
    return pl.pallas_call(
        score_kernel,
        out_shape=jax.ShapeDtypeStruct((slots, 128), jnp.float32),
        grid_spec=pltpu.PrefetchScalarGridSpec(
            num_scalar_prefetch=2, grid=(slots // GROUP,),
            in_specs=[full(arr) for arr in args],
            out_specs=pl.BlockSpec((GROUP, 128), lambda i, *_: (i, 0))),
        compiler_params=pltpu.CompilerParams(vmem_limit_bytes=40 << 20),
        name="score_items",
    )(pidx, ridx, *args)


def mirror_matrix(frequency_total):
    turn = np.zeros((2 * frequency_total, 2 * frequency_total), np.float32)
    for c in range(1, frequency_total):
        turn[frequency_total - c, c] = 1.0
        turn[2 * frequency_total - c, frequency_total + c] = -1.0
    return turn


def half_spectra(images, defocus, frequency_total, lines):
    side = images.shape[-1]
    half = frequency_total // 2
    freqs = np.arange(frequency_total) - half
    ang = 2 * np.pi * ((np.arange(side)[:, None] * freqs[None, :]) % side) / side
    cos, sin = np.cos(ang).astype(np.float32), np.sin(ang).astype(np.float32)
    first = jnp.einsum("pyx,xf->pyf", images, np.concatenate([cos, -sin], axis=1), precision=HALF_PRECISION)
    both = jnp.concatenate(
        [first, jnp.concatenate([first[..., frequency_total:], -first[..., :frequency_total]], axis=2)], axis=1)
    rows = np.zeros((lines, 2 * side), np.float32)
    rows[: half + 1] = np.concatenate([cos[:, : half + 1].T, sin[:, : half + 1].T], axis=1)
    spectra = jnp.einsum("ry,pyg->prg", rows, both, precision=HALF_PRECISION)
    edge_in = jnp.concatenate([first[:, :, 0], first[:, :, frequency_total]], axis=1)
    back = np.zeros((side, frequency_total), np.float32), np.zeros((side, frequency_total), np.float32)
    for r in range(1, half + 1):
        back[0][:, r], back[1][:, r] = cos[:, frequency_total - r] if r < half else cos[:, half], (
            sin[:, frequency_total - r] if r < half else sin[:, half])
    edge = jnp.dot(edge_in, np.block([[back[0], back[1]], [back[1], -back[0]]]), precision=HALF_PRECISION)
    f = freqs.astype(np.float32)
    fr = np.zeros((lines,), np.float32)
    fr[: half + 1] = f[: half + 1]
    radius = (fr[:, None] ** 2 + f[None, :] ** 2) / float(half * half)
    radius[half + 1] = radius[0]
    radius[half + 1, 1:half + 1] = radius[0][(frequency_total - np.arange(1, half + 1)) % frequency_total]
    phase = defocus[:, None, None] * radius[None]
    factor = -(math.sqrt(1.0 - AMPLITUDE * AMPLITUDE) * jnp.sin(phase) + AMPLITUDE * jnp.cos(phase)) / side
    value = spectra + edge[:, None, :] * (np.arange(lines) == half + 1).astype(np.float32)[None, :, None]
    return value * jnp.concatenate([factor, factor], axis=2)


def fold_references(references, lines):
    frequency_total = references.shape[1]
    half = frequency_total // 2
    sign = np.concatenate([np.ones(frequency_total), -np.ones(frequency_total)]).astype(np.float32)
    turned = jnp.einsum("rab,bc->rac", references[:, :half:-1], mirror_matrix(frequency_total) * sign[None, :],
                        precision=HIGH_PRECISION)
    folded = references[:, : half + 1] * sign
    folded = folded + jnp.pad(turned, ((0, 0), (1, 1), (0, 0)))
    edge = jnp.concatenate(
        [jnp.pad(references[:, :half:-1, col], ((0, 0), (1, frequency_total - half)))
         for col in (0, frequency_total)], axis=1)
    folded = jnp.concatenate(
        [folded, edge[:, None, :], jnp.zeros((references.shape[0], lines - half - 2, 2 * frequency_total))], axis=1)
    re, im = folded[..., :frequency_total], folded[..., frequency_total:]
    return jnp.concatenate([re, re], axis=2), jnp.concatenate([-im, im], axis=2)


def gather_device(images, defocus, references, orient_owner, orient_local, block_owner, block_cell):
    count = lax.axis_size("slab")
    me = lax.axis_index("slab")
    side = images.shape[-1]
    frequency_total = references.shape[1]
    half = frequency_total // 2
    parts, picks = orient_owner.shape
    refs, bands = block_cell.shape
    items = parts * picks
    cells = ZDEV * (VY // (frequency_total // bands)) * (VX // frequency_total)
    band_rows = frequency_total // bands
    cap = max(2, 2 * items // count)
    lines = 40
    meta_row = half + 2
    own = half_spectra(images, defocus, frequency_total, lines)
    ids = (orient_owner * refs + orient_local).astype(jnp.float32)
    codes = (block_owner[..., 0] * cells + block_cell).astype(jnp.float32).reshape(parts, -1)
    meta = jnp.concatenate([ids, codes], axis=1)
    meta = jnp.pad(meta, ((0, 0), (0, 2 * frequency_total - meta.shape[1])))
    own = jnp.where((jnp.arange(lines) == meta_row)[None, :, None], meta[:, None, :], own)
    ref_a, ref_b = fold_references(references, lines)
    gathered = ring_gather(own, count)
    flat = gathered.reshape(count * parts, lines, 2 * frequency_total)
    meta = flat[:, meta_row]
    ids = meta[:, :picks].astype(jnp.int32)
    codes = meta[:, picks:picks + refs * bands // parts].astype(jnp.int32).reshape(count * refs, bands)
    by_source = ids.reshape(count, items)
    owner = by_source // refs
    same = owner[:, :, None] == owner[:, None, :]
    before = np.tril(np.ones((items, items), bool), -1)
    rank = jnp.sum(jnp.where(same & before[None], 1, 0), axis=2)
    mine = (owner == me)[:, :, None] & (rank[:, :, None] == jnp.arange(cap)[None, None, :])
    particle = (jnp.arange(count)[:, None] * parts + jnp.arange(items)[None, :] // picks)
    pick = lambda value: jnp.sum(jnp.where(mine, value[:, :, None], 0), axis=1).reshape(-1)
    pidx, ridx = pick(particle), pick(by_source % refs)
    peaks = score_items(pidx, ridx, flat, ref_a, ref_b, side, frequency_total)[:, 0]
    slot_scores = peaks * peaks + EPSILON
    everyone = share(jnp.broadcast_to(slot_scores[None], (8, count * cap)), count)[:, 0]
    table = everyone.reshape(count, count, cap).transpose(1, 0, 2).reshape(count, count * cap)
    where = owner * cap + rank
    scores = jnp.sum(
        jnp.where(where[:, :, None] == jnp.arange(count * cap)[None, None, :], table[:, None, :], 0.0), axis=2)
    scores = scores.reshape(count * parts, picks)
    posterior = scores / jnp.sum(scores, axis=1, keepdims=True)
    weight = jnp.zeros((count * refs, count * parts), jnp.float32)
    for k in range(picks):
        weight = weight + jnp.where(
            jnp.arange(count * refs)[:, None] == ids[None, :, k], posterior[None, :, k], 0.0)
    place = (codes.T[:, None, :] == (me * cells + jnp.arange(cells))[None, :, None]).astype(jnp.bfloat16)
    w_hi = lax.reduce_precision(weight, 8, 7)
    w_low = lax.reduce_precision(weight - w_hi, 8, 7)
    mix = jnp.einsum("jcr,rp->jcp", place, jnp.concatenate([w_hi, w_low], axis=1).astype(jnp.bfloat16),
                     preferred_element_type=jnp.float32)
    n = count * parts
    mix = mix[..., :n] + mix[..., n:]
    halves = bands // 2
    direct = jnp.einsum("jcp,pjil->cil", mix[:halves],
                        flat[:, :half].reshape(n, halves, band_rows, 2 * frequency_total), precision=HALF_PRECISION)
    mixed = mix[halves:][::-1]
    back = jnp.einsum("jcp,pjil->cil", mixed,
                      flat[:, 1:half + 1].reshape(n, halves, band_rows, 2 * frequency_total), precision=HALF_PRECISION)
    edge = flat[:, half + 1].reshape(n, 2, frequency_total)[:, :, 1:half + 1].reshape(n, 2, halves, band_rows)
    edge = jnp.einsum("jcp,ptji->cit", mixed, edge, precision=HALF_PRECISION)
    back = jnp.einsum("cil,lm->cim", back, mirror_matrix(frequency_total), precision=HIGH_PRECISION)
    lane = np.arange(2 * frequency_total)
    back = back + jnp.where(lane == 0, edge[..., 0:1], 0.0) - jnp.where(lane == frequency_total, edge[..., 1:2], 0.0)
    total = direct + back[:, ::-1]
    row_blocks, col_blocks = VY // band_rows, VX // frequency_total
    span = row_blocks // 2
    total = total.reshape(ZDEV, 2, span, col_blocks, band_rows, 2 * frequency_total)
    axis = lax.axis_index("dp")
    mine_half = lax.dynamic_index_in_dim(total, axis, 1, keepdims=False)
    peer_half = lax.dynamic_index_in_dim(total, 1 - axis, 1, keepdims=False)
    summed = mine_half + lax.ppermute(peer_half, "dp", [(0, 1), (1, 0)])
    summed = summed.reshape(ZDEV, span, col_blocks, band_rows, 2, frequency_total)
    volume = summed.transpose(0, 1, 3, 4, 2, 5).reshape(ZDEV, span * band_rows, 2, col_blocks * frequency_total)
    own_posterior = lax.dynamic_slice_in_dim(posterior, me * parts, parts, axis=0)
    return (own_posterior, volume)


def solution(mesh):
    in_specs = (
        P(("dp", "slab"), None, None),
        P(("dp", "slab")),
        P("slab", None, None),
        P(("dp", "slab"), None),
        P(("dp", "slab"), None),
        P("slab", None, None),
        P("slab", None),
    )
    out_specs = (P(("dp", "slab"), None), P("slab", "dp", None, None))
    small = mesh.shape["dp"] == 2 and mesh.shape["slab"] == 16
    return jax.shard_map(
        gather_device if small else per_device, mesh=mesh, in_specs=in_specs, out_specs=out_specs, check_vma=False
    )
```

```python
import functools
import math

import jax
import jax.numpy as jnp
import numpy as np
from jax import lax
from jax.experimental import pallas as pl
from jax.experimental.pallas import tpu as pltpu
from jax.sharding import PartitionSpec as P

VY = 256
VX = 256
ZDEV = 4


HIGH_PRECISION = lax.Precision.HIGHEST
AMPLITUDE = 0.1
EPSILON = 1e-05


def freq_tables(image_side, frequency_total):
    pixels = jnp.arange(image_side, dtype=jnp.int32)
    freqs = jnp.arange(frequency_total, dtype=jnp.int32) - frequency_total // 2
    phase = jnp.mod(pixels[:, None] * freqs[None, :], image_side).astype(jnp.float32) * (
        2.0 * math.pi / image_side
    )
    return (jnp.cos(phase), jnp.sin(phase))


def contrast(defocus, frequency_total):
    freqs = (jnp.arange(frequency_total, dtype=jnp.int32) - frequency_total // 2).astype(
        jnp.float32
    )
    radius = (freqs[:, None] * freqs[:, None] + freqs[None, :] * freqs[None, :]) / float(
        (frequency_total // 2) ** 2
    )
    phase = defocus[:, None, None] * radius[None]
    return -(math.sqrt(1.0 - AMPLITUDE * AMPLITUDE) * jnp.sin(phase) + AMPLITUDE * jnp.cos(phase))


def spectra_of(images, defocus, frequency_total):
    image_side = images.shape[-1]
    cosine, sine = freq_tables(image_side, frequency_total)
    first_pass = jnp.einsum(
        "pyx,xf->pyf", images, jnp.concatenate([cosine, -sine], axis=1), precision=HIGH_PRECISION
    )
    lower_half = jnp.concatenate(
        [first_pass[..., frequency_total:], -first_pass[..., :frequency_total]], axis=2
    )
    spectra = jnp.einsum("yf,pyg->pfg", cosine, first_pass, precision=HIGH_PRECISION) + jnp.einsum(
        "yf,pyg->pfg", sine, lower_half, precision=HIGH_PRECISION
    )
    factor = contrast(defocus, frequency_total) / image_side
    return spectra * jnp.concatenate([factor, factor], axis=2)


def score_slots(chosen, received, image_side):
    frequency_total = received.shape[1]
    cosine, sine = freq_tables(image_side, frequency_total)
    rotation_angle = jnp.concatenate(
        [jnp.concatenate([cosine.T, sine.T], axis=1), jnp.concatenate([-sine.T, cosine.T], axis=1)],
        axis=0,
    )
    inverted_rows = jnp.concatenate([cosine, -sine], axis=1)
    slot_total = received.shape[0]
    group_size = math.gcd(slot_total, 16)

    def one_group(couple):
        ref_part, spec_part = couple
        ref_re, ref_im = (ref_part[..., :frequency_total], ref_part[..., frequency_total:])
        spec_re, spec_im = (spec_part[..., :frequency_total], spec_part[..., frequency_total:])
        spectral_product = jnp.concatenate(
            [ref_re * spec_re + ref_im * spec_im, ref_re * spec_im - ref_im * spec_re], axis=2
        )
        center_index = jnp.einsum(
            "eio,ol->eil", spectral_product, rotation_angle, precision=HIGH_PRECISION
        )
        stacked_planes = jnp.concatenate(
            [center_index[..., :image_side], center_index[..., image_side:]], axis=1
        )
        translation_offsets = (
            jnp.einsum("kz,wzq->wkq", inverted_rows, stacked_planes, precision=HIGH_PRECISION)
            / frequency_total
        )
        return (
            jnp.max(
                (translation_offsets * translation_offsets).reshape(
                    translation_offsets.shape[0], -1
                ),
                axis=1,
            )
            + EPSILON
        )

    grouped = (
        chosen.reshape((slot_total // group_size, group_size) + chosen.shape[1:]),
        received.reshape((slot_total // group_size, group_size) + received.shape[1:]),
    )
    return lax.map(one_group, grouped).reshape(-1)


def slot_ranks(owner_ids, owner_count):
    owner_hits = (owner_ids[:, None] == jnp.arange(owner_count, dtype=jnp.int32)[None, :]).astype(
        jnp.int32
    )
    return jnp.sum((jnp.cumsum(owner_hits, axis=0) - 1) * owner_hits, axis=1)


def insert(blocks, cell_ids, planes, row_blocks, col_blocks, first_block, span_blocks):
    band_rows, row_width = (blocks.shape[2], blocks.shape[3])
    frequency_total = row_width // 2
    flat_rows = blocks.reshape(-1, band_rows * row_width)
    cell_ids = cell_ids.reshape(-1)
    plane_of = cell_ids // (row_blocks * col_blocks)
    row_of = cell_ids // col_blocks % row_blocks - first_block
    column_of = cell_ids % col_blocks
    usable = (cell_ids >= 0) & (row_of >= 0) & (row_of < span_blocks)
    target = jnp.where(usable, (plane_of * span_blocks + row_of) * col_blocks + column_of, -1)
    placing = (
        jnp.arange(planes * span_blocks * col_blocks, dtype=jnp.int32)[:, None] == target[None, :]
    ).astype(jnp.float32)
    placed = jnp.dot(placing, flat_rows, precision=HIGH_PRECISION)
    placed = placed.reshape(planes, span_blocks, col_blocks, band_rows, 2, frequency_total)
    return placed.transpose(0, 1, 3, 4, 2, 5).reshape(
        planes, span_blocks * band_rows, 2, col_blocks * frequency_total
    )


def per_device(images, defocus, references, orient_owner, orient_local, block_owner, block_cell):
    owner_count = lax.axis_size("slab")
    frequency_total = references.shape[1]
    image_side = images.shape[-1]
    part_count, pick_count = orient_owner.shape
    ref_rows = references.shape[0]
    slot_cap = max(2, 2 * part_count * pick_count // owner_count)
    spectra = spectra_of(images, defocus, frequency_total)
    flat_owner = orient_owner.reshape(-1)
    slot_of = flat_owner * slot_cap + slot_ranks(flat_owner, owner_count)
    particle_of = jnp.arange(part_count * pick_count, dtype=jnp.int32) // pick_count
    send_spectra = jnp.zeros(
        (owner_count * slot_cap, frequency_total, 2 * frequency_total), jnp.float32
    )
    send_spectra = send_spectra.at[slot_of].set(jnp.repeat(spectra, pick_count, axis=0))
    send_meta = jnp.full((owner_count * slot_cap, 2), -1, jnp.int32)
    send_meta = send_meta.at[slot_of].set(
        jnp.stack([orient_local.reshape(-1), particle_of], axis=1)
    )
    received, meta_in = (
        lax.all_to_all(
            send_spectra.reshape(owner_count, slot_cap, frequency_total, 2 * frequency_total),
            "slab",
            split_axis=0,
            concat_axis=0,
            tiled=True,
        ),
        lax.all_to_all(
            send_meta.reshape(owner_count, slot_cap, 2),
            "slab",
            split_axis=0,
            concat_axis=0,
            tiled=True,
        ),
    )
    flat_received = received.reshape(-1, frequency_total, 2 * frequency_total)
    ref_index = meta_in[..., 0].reshape(-1)
    chosen = references[jnp.clip(ref_index, 0, ref_rows - 1)]
    scores = score_slots(chosen, flat_received, image_side)
    slot_scores = scores.reshape(owner_count, slot_cap)
    back_scores = lax.all_to_all(slot_scores, "slab", split_axis=0, concat_axis=0, tiled=True)
    item_scores = back_scores.reshape(-1)[slot_of].reshape(part_count, pick_count)
    posterior = item_scores / jnp.sum(item_scores, axis=1, keepdims=True)
    slot_weight = (
        jnp.zeros((owner_count * slot_cap,), jnp.float32).at[slot_of].set(posterior.reshape(-1))
    )
    got_weight = lax.all_to_all(
        slot_weight.reshape(owner_count, slot_cap), "slab", split_axis=0, concat_axis=0, tiled=True
    ).reshape(-1)
    ref_hits = (ref_index[None, :] == jnp.arange(ref_rows, dtype=jnp.int32)[:, None]).astype(
        jnp.float32
    ) * got_weight[None, :]
    averages = jnp.dot(
        ref_hits, flat_received.reshape(flat_received.shape[0], -1), precision=HIGH_PRECISION
    )
    averages = averages.reshape(ref_rows, frequency_total, 2 * frequency_total)
    bands = block_cell.shape[1]
    band_rows = frequency_total // bands
    block_cap = max(2, 2 * ref_rows * bands // owner_count)
    dest_owner = block_owner.reshape(-1)
    block_slot = dest_owner * block_cap + slot_ranks(dest_owner, owner_count)
    cell_send = (
        jnp.full((owner_count * block_cap,), -1, jnp.int32)
        .at[block_slot]
        .set(block_cell.reshape(-1))
    )
    row_blocks = VY // band_rows
    col_blocks = VX // frequency_total
    pieces = averages.reshape(ref_rows * bands, band_rows, 2 * frequency_total)
    block_send = (
        jnp.zeros((owner_count * block_cap, band_rows, 2 * frequency_total), jnp.float32)
        .at[block_slot]
        .set(pieces)
    )
    blocks_in = lax.all_to_all(
        block_send.reshape(owner_count, block_cap, band_rows, 2 * frequency_total),
        "slab",
        split_axis=0,
        concat_axis=0,
        tiled=True,
    )
    cells_in = lax.all_to_all(
        cell_send.reshape(owner_count, block_cap), "slab", split_axis=0, concat_axis=0, tiled=True
    )
    partial_value = insert(blocks_in, cells_in, ZDEV, row_blocks, col_blocks, 0, row_blocks)
    volume = lax.psum_scatter(partial_value, "dp", scatter_dimension=1, tiled=True)
    return (posterior, volume)


HALF_PRECISION = lax.Precision.HIGH
MESH = pl.DeviceIdType.MESH


def ring_place(pos, depth):
    back = pos // depth
    z = (1 - back) * pos + back * (2 * depth - 1 - pos)
    return z * 2 + back


def gather_kernel(chips, own_ref, out_ref, local_sem, ring_send, ring_recv, pair_send, pair_recv):
    depth = chips // 2
    me = lax.axis_index("slab")
    core = me % 2
    chip = me // 2
    z, back = chip // 2, chip % 2
    pos = z + back * (2 * depth - 1 - 2 * z)
    dirs = ((pos + 1) % chips, (pos + chips - 1) % chips)
    targets = [ring_place(q, depth) * 2 + core for q in dirs]
    sibling = chip * 2 + 1 - core
    barrier = pltpu.get_barrier_semaphore()
    for other in targets + [sibling]:
        pl.semaphore_signal(barrier, inc=1, device_id={"slab": other}, device_id_type=MESH)
    pl.semaphore_wait(barrier, 3)
    part = own_ref.shape[0] // 2
    rows = lambda ref, h: ref.at[pl.ds(h * part, part)]
    local = pltpu.make_async_copy(own_ref, out_ref.at[me], local_sem)
    local.start()
    waits = []

    def ring_copy(src, origin, d, t, h):
        return pltpu.make_async_remote_copy(
            src_ref=src, dst_ref=rows(out_ref.at[origin], h),
            send_sem=ring_send.at[d, t, h], recv_sem=ring_recv.at[d, t, h],
            device_id={"slab": targets[d]}, device_id_type=MESH)

    def pair_copy(src, origin, n, h):
        return pltpu.make_async_remote_copy(
            src_ref=src, dst_ref=rows(out_ref.at[origin], h),
            send_sem=pair_send.at[n, h], recv_sem=pair_recv.at[n, h],
            device_id={"slab": sibling}, device_id_type=MESH)

    def origin_of(d, t):
        q = (pos + chips - t) % chips if d == 0 else (pos + t) % chips
        return ring_place(q, depth) * 2 + core

    hops = [(d, t, h) for t in range(depth) for h in range(2) for d in range(2)
            if t < depth - 1 or h == d]
    pair_of = lambda d, t, h: (t + 1 if d == 0 else depth + t + 1) if t < depth - 1 else depth
    for d, t, h in hops:
        if t == 0:
            copy = ring_copy(rows(own_ref, h), me, d, 0, h)
            copy.start()
            waits.append(copy)
    for h in range(2):
        copy = pair_copy(rows(own_ref, h), me, 0, h)
        copy.start()
        waits.append(copy)
    pairs = []
    for d, t, h in hops:
        origin = origin_of(d, t + 1)
        landed = rows(out_ref.at[origin], h)
        ring_copy(landed, origin, d, t, h).wait_recv()
        if (d, t + 1, h) in hops:
            copy = ring_copy(landed, origin, d, t + 1, h)
            copy.start()
            waits.append(copy)
        copy = pair_copy(landed, origin, pair_of(d, t, h), h)
        copy.start()
        pairs.append(copy)
        waits.append(copy)
    for copy in waits:
        copy.wait_send()
    pair_copy(rows(own_ref, 0), me, 0, 0).wait_recv()
    pair_copy(rows(own_ref, 1), me, 0, 1).wait_recv()
    for copy in pairs:
        copy.wait_recv()
    local.wait()


def ring_gather(payload, owner_count):
    chips = owner_count // 2
    depth = chips // 2
    return pl.pallas_call(
        functools.partial(gather_kernel, chips),
        out_shape=jax.ShapeDtypeStruct((owner_count,) + payload.shape, payload.dtype),
        in_specs=[pl.BlockSpec(memory_space=pl.ANY)],
        out_specs=pl.BlockSpec(memory_space=pl.ANY),
        scratch_shapes=[
            pltpu.SemaphoreType.DMA,
            pltpu.SemaphoreType.DMA((2, depth, 2)),
            pltpu.SemaphoreType.DMA((2, depth, 2)),
            pltpu.SemaphoreType.DMA((chips, 2)),
            pltpu.SemaphoreType.DMA((chips, 2)),
        ],
        compiler_params=pltpu.CompilerParams(collective_id=1, has_side_effects=True),
        name="ring_gather",
    )(payload)


def share_kernel(count, own_ref, out_ref, local_sem, send_sem, recv_sem):
    me = lax.axis_index("slab")
    barrier = pltpu.get_barrier_semaphore()
    others = [(me + step) % count for step in range(1, count)]
    for other in others:
        pl.semaphore_signal(barrier, inc=1, device_id={"slab": other}, device_id_type=MESH)
    local = pltpu.make_async_copy(own_ref, out_ref.at[me], local_sem)
    local.start()
    pl.semaphore_wait(barrier, count - 1)
    copies = []
    for n, other in enumerate(others):
        copy = pltpu.make_async_remote_copy(
            src_ref=own_ref, dst_ref=out_ref.at[me], send_sem=send_sem.at[n],
            recv_sem=recv_sem.at[n], device_id={"slab": other}, device_id_type=MESH)
        copy.start()
        copies.append(copy)
    for n, copy in enumerate(copies):
        copy.wait_send()
        source = (me + count - 1 - n) % count
        pltpu.make_async_remote_copy(
            src_ref=own_ref, dst_ref=out_ref.at[source], send_sem=send_sem.at[n],
            recv_sem=recv_sem.at[n], device_id={"slab": source}, device_id_type=MESH).wait_recv()
    local.wait()


def share(row, count):
    return pl.pallas_call(
        functools.partial(share_kernel, count),
        out_shape=jax.ShapeDtypeStruct((count,) + row.shape, row.dtype),
        in_specs=[pl.BlockSpec(memory_space=pltpu.VMEM)],
        out_specs=pl.BlockSpec(memory_space=pltpu.VMEM),
        scratch_shapes=[
            pltpu.SemaphoreType.DMA,
            pltpu.SemaphoreType.DMA((count - 1,)),
            pltpu.SemaphoreType.DMA((count - 1,)),
        ],
        compiler_params=pltpu.CompilerParams(collective_id=2, has_side_effects=True),
        name="share_scores",
    )(row)


GROUP = 8


def score_kernel(pidx, ridx, half_ref, a_ref, b_ref, whi_ref, wlo_ref, cc_ref, pat_ref, out_ref):
    step = pl.program_id(0)
    lines = half_ref.shape[1]
    f32, bf16 = jnp.float32, jnp.bfloat16
    products = []
    for e in range(GROUP):
        spec = half_ref[pidx[step * GROUP + e]]
        ref = ridx[step * GROUP + e]
        products.append(a_ref[ref] * spec + b_ref[ref] * pltpu.roll(spec, 64, 1))
    product = jnp.concatenate(products, axis=0)
    hi = product.astype(bf16)
    lo = (product - hi.astype(f32)).astype(bf16)
    dot = lambda x, y: jnp.dot(x, y, preferred_element_type=f32)
    turned = dot(hi, whi_ref[...]) + dot(lo, whi_ref[...]) + dot(hi, wlo_ref[...])
    edge = jnp.concatenate([p[33:34] for p in products], axis=0).T
    cosine, sine = pat_ref[0:1], pat_ref[1:2]
    stacks = []
    for e in range(GROUP):
        rows = turned[e * lines:(e + 1) * lines]
        er, ei = edge[0:lines, e:e + 1], edge[64:64 + lines, e:e + 1]
        both = jnp.concatenate(
            [rows[:, :128] + er * cosine - ei * sine, rows[:, 128:] + er * sine + ei * cosine], axis=0)
        high = both.astype(bf16)
        low = (both - high.astype(f32)).astype(bf16)
        stacks.append(jnp.concatenate([high, low, high], axis=0))
    peaks = []
    for e in range(0, GROUP, 2):
        shifts = jnp.abs(dot(cc_ref[...], jnp.concatenate(stacks[e:e + 2], axis=1)))
        best = jnp.max(shifts, axis=0, keepdims=True)
        peaks += [best[:, :128], best[:, 128:]]
    peak = jnp.max(jnp.concatenate(peaks, axis=0), axis=1, keepdims=True)
    out_ref[...] = jnp.broadcast_to(peak, (GROUP, 128))


def score_tables(image_side, frequency_total, lines):
    half = frequency_total // 2
    x = np.arange(image_side)
    freqs = np.arange(frequency_total) - half
    ang = 2 * np.pi * ((freqs[:, None] * x[None, :]) % image_side) / image_side
    cos, sin = np.cos(ang), np.sin(ang)
    w = np.block([[cos, sin], [-sin, cos]]) / frequency_total
    cr, sr = np.zeros((image_side, lines)), np.zeros((image_side, lines))
    cr[:, : half + 1], sr[:, : half + 1] = cos[: half + 1].T, sin[: half + 1].T
    c = np.concatenate([cr, -sr], axis=1)
    def two(m):
        high = m.astype(jnp.bfloat16)
        return high, (m - high.astype(np.float64)).astype(jnp.bfloat16)
    whi, wlo = two(w)
    chi, clo = two(c)
    pat = np.zeros((8, image_side), np.float32)
    pat[0] = np.array([1, 0, -1, 0])[x % 4] / frequency_total
    pat[1] = np.array([0, 1, 0, -1])[x % 4] / frequency_total
    return whi, wlo, np.concatenate([chi, chi, clo], axis=1), pat


def score_items(pidx, ridx, spectra, ref_a, ref_b, image_side, frequency_total):
    slots = pidx.shape[0]
    lines = spectra.shape[1]
    whi, wlo, cc, pat = (jnp.asarray(t) for t in score_tables(image_side, frequency_total, lines))
    full = lambda arr: pl.BlockSpec(arr.shape, lambda i, *_: (0,) * arr.ndim, pipeline_mode=pl.Buffered(1))
    args = (spectra, ref_a, ref_b, whi, wlo, cc, pat)
    return pl.pallas_call(
        score_kernel,
        out_shape=jax.ShapeDtypeStruct((slots, 128), jnp.float32),
        grid_spec=pltpu.PrefetchScalarGridSpec(
            num_scalar_prefetch=2, grid=(slots // GROUP,),
            in_specs=[full(arr) for arr in args],
            out_specs=pl.BlockSpec((GROUP, 128), lambda i, *_: (i, 0))),
        compiler_params=pltpu.CompilerParams(vmem_limit_bytes=40 << 20),
        name="score_items",
    )(pidx, ridx, *args)


def mirror_matrix(frequency_total):
    turn = np.zeros((2 * frequency_total, 2 * frequency_total), np.float32)
    for c in range(1, frequency_total):
        turn[frequency_total - c, c] = 1.0
        turn[2 * frequency_total - c, frequency_total + c] = -1.0
    return turn


def half_spectra(images, defocus, frequency_total, lines):
    side = images.shape[-1]
    half = frequency_total // 2
    freqs = np.arange(frequency_total) - half
    ang = 2 * np.pi * ((np.arange(side)[:, None] * freqs[None, :]) % side) / side
    cos, sin = np.cos(ang).astype(np.float32), np.sin(ang).astype(np.float32)
    first = jnp.einsum("pyx,xf->pyf", images, np.concatenate([cos, -sin], axis=1), precision=HALF_PRECISION)
    both = jnp.concatenate(
        [first, jnp.concatenate([first[..., frequency_total:], -first[..., :frequency_total]], axis=2)], axis=1)
    rows = np.zeros((lines, 2 * side), np.float32)
    rows[: half + 1] = np.concatenate([cos[:, : half + 1].T, sin[:, : half + 1].T], axis=1)
    spectra = jnp.einsum("ry,pyg->prg", rows, both, precision=HALF_PRECISION)
    edge_in = jnp.concatenate([first[:, :, 0], first[:, :, frequency_total]], axis=1)
    back = np.zeros((side, frequency_total), np.float32), np.zeros((side, frequency_total), np.float32)
    for r in range(1, half + 1):
        back[0][:, r], back[1][:, r] = cos[:, frequency_total - r] if r < half else cos[:, half], (
            sin[:, frequency_total - r] if r < half else sin[:, half])
    edge = jnp.dot(edge_in, np.block([[back[0], back[1]], [back[1], -back[0]]]), precision=HALF_PRECISION)
    f = freqs.astype(np.float32)
    fr = np.zeros((lines,), np.float32)
    fr[: half + 1] = f[: half + 1]
    radius = (fr[:, None] ** 2 + f[None, :] ** 2) / float(half * half)
    radius[half + 1] = radius[0]
    radius[half + 1, 1:half + 1] = radius[0][(frequency_total - np.arange(1, half + 1)) % frequency_total]
    phase = defocus[:, None, None] * radius[None]
    factor = -(math.sqrt(1.0 - AMPLITUDE * AMPLITUDE) * jnp.sin(phase) + AMPLITUDE * jnp.cos(phase)) / side
    value = spectra + edge[:, None, :] * (np.arange(lines) == half + 1).astype(np.float32)[None, :, None]
    return value * jnp.concatenate([factor, factor], axis=2)


def fold_references(references, lines):
    frequency_total = references.shape[1]
    half = frequency_total // 2
    sign = np.concatenate([np.ones(frequency_total), -np.ones(frequency_total)]).astype(np.float32)
    turned = jnp.einsum("rab,bc->rac", references[:, :half:-1], mirror_matrix(frequency_total) * sign[None, :],
                        precision=HIGH_PRECISION)
    folded = references[:, : half + 1] * sign
    folded = folded + jnp.pad(turned, ((0, 0), (1, 1), (0, 0)))
    edge = jnp.concatenate(
        [jnp.pad(references[:, :half:-1, col], ((0, 0), (1, frequency_total - half)))
         for col in (0, frequency_total)], axis=1)
    folded = jnp.concatenate(
        [folded, edge[:, None, :], jnp.zeros((references.shape[0], lines - half - 2, 2 * frequency_total))], axis=1)
    re, im = folded[..., :frequency_total], folded[..., frequency_total:]
    return jnp.concatenate([re, re], axis=2), jnp.concatenate([-im, im], axis=2)


def volume_kernel(cidx_ref, post_ref, flat_ref, turn_ref, out_ref,
                  s_hi, s_lo, m_hi, m_lo, edge, away, inbox, send_sem, recv_sem):
    f32, bf16 = jnp.float32, jnp.bfloat16
    picks, n = post_ref.shape
    lines = flat_ref.shape[0] // n
    bands, halves = m_hi.shape[1], m_hi.shape[1] // 2
    peer = 1 - lax.axis_index("dp")
    barrier = pltpu.get_barrier_semaphore()
    pl.semaphore_signal(barrier, inc=1, device_id={"dp": peer}, device_id_type=MESH)

    def split(value):
        high = value.astype(bf16)
        return high, (value - high.astype(f32)).astype(bf16)

    for row in range(s_hi.shape[0]):
        s_hi[row], s_lo[row] = split(flat_ref[pl.ds(row, n, stride=lines), :])

    def build(j, carry):
        where = cidx_ref[pl.ds(j, 1), :]
        for part in range(2):
            cell = lax.broadcasted_iota(jnp.int32, (n, n), 0) + part * n
            total = jnp.zeros((n, n), f32)
            for k in range(picks):
                total = total + jnp.where(where[:, k * n:(k + 1) * n] == cell, post_ref[k:k + 1, :], 0.0)
            m_hi[part, j], m_lo[part, j] = split(total)
        return carry

    lax.fori_loop(0, bands, build, 0)
    pl.semaphore_wait(barrier, 1)

    def dot(x, y):
        return jnp.dot(x, y, preferred_element_type=f32)

    def product(part, j, hi, lo):
        return dot(m_hi[part, j], hi) + dot(m_lo[part, j], hi) + dot(m_hi[part, j], lo)

    last = s_hi.shape[0] - 1
    lane = lax.broadcasted_iota(jnp.int32, (n, 128), 1)

    def edges(part):
        total = jnp.zeros((n, 128), f32)
        ext = flat_ref[pl.ds(last, n, stride=lines), :]
        for jj in range(halves):
            hi, lo = split(pltpu.roll(ext, 128 - (1 + 8 * jj), 1))
            total = total + product(part, bands - 1 - jj, hi, lo)
        edge[...] = total

    def pair(ref, first, second):
        return jnp.concatenate([ref[first], ref[second]], axis=1)

    def chunk(part, ip):
        i = 2 * ip
        front, back = jnp.zeros((n, 256), f32), jnp.zeros((n, 256), f32)
        for jj in range(halves):
            a, b = 8 * jj + i, 8 * jj + i + 1
            front = front + product(part, jj, pair(s_hi, a, b), pair(s_lo, a, b))
            a, b = 8 * jj + 8 - i, 8 * jj + 7 - i
            back = back + product(part, bands - 1 - jj, pair(s_hi, a, b), pair(s_lo, a, b))
        result = []
        for u in range(2):
            hi, lo = split(back[:, u * 128:(u + 1) * 128])
            flipped = dot(hi, turn_ref[...]) + dot(lo, turn_ref[...])
            at = pltpu.roll(edge[...], (128 - (7 - i - u)) % 128, 1)
            flipped = flipped + jnp.where(lane == 0, at, jnp.where(lane == 64, -at, 0.0))
            full = front[:, u * 128:(u + 1) * 128] + flipped
            rolled = pltpu.roll(full, 64, 1)
            q = n // 4
            low = lane[:q] < 64
            for p in range(2):
                x, y = slice(2 * p * q, (2 * p + 1) * q), slice((2 * p + 1) * q, (2 * p + 2) * q)
                result.append((u, p, jnp.where(low, full[x], rolled[y])))
                result.append((u, 2 + p, jnp.where(low, rolled[x], full[y])))
        return result

    def copy_of(ip):
        return pltpu.make_async_remote_copy(
            src_ref=away.at[ip], dst_ref=inbox.at[ip], send_sem=send_sem.at[ip], recv_sem=recv_sem.at[ip],
            device_id={"dp": peer}, device_id_type=MESH)

    pieces = away.shape[0]
    edges(0)
    for ip in range(pieces):
        for u, p, value in chunk(0, ip):
            away[ip, u, p] = value
        copy_of(ip).start()
    edges(1)
    for ip in range(pieces):
        for u, p, value in chunk(1, ip):
            out_ref[ip, u, p] = value
    for ip in range(pieces):
        copy_of(ip).wait_recv()
        out_ref[ip] = out_ref[ip] + inbox[ip]
    for ip in range(pieces):
        copy_of(ip).wait_send()


def build_volume(cidx, post, flat, half):
    bands, n = cidx.shape[0], post.shape[1]
    lanes = flat.shape[1]
    turn = jnp.asarray(mirror_matrix(lanes // 2), jnp.bfloat16)
    piece = (4, 2, 4, n // 4, lanes)
    vmem = pl.BlockSpec(memory_space=pltpu.VMEM)
    return pl.pallas_call(
        volume_kernel,
        out_shape=jax.ShapeDtypeStruct(piece, jnp.float32),
        in_specs=[vmem] * 4,
        out_specs=vmem,
        scratch_shapes=[
            pltpu.VMEM((half + 2, n, lanes), jnp.bfloat16),
            pltpu.VMEM((half + 2, n, lanes), jnp.bfloat16),
            pltpu.VMEM((2, bands, n, n), jnp.bfloat16),
            pltpu.VMEM((2, bands, n, n), jnp.bfloat16),
            pltpu.VMEM((n, lanes), jnp.float32),
            pltpu.VMEM(piece, jnp.float32),
            pltpu.VMEM(piece, jnp.float32),
            pltpu.SemaphoreType.DMA((4,)),
            pltpu.SemaphoreType.DMA((4,)),
        ],
        compiler_params=pltpu.CompilerParams(
            collective_id=3, has_side_effects=True, vmem_limit_bytes=48 << 20),
        name="build_volume",
    )(cidx, post, flat, turn)


def gather_device(images, defocus, references, orient_owner, orient_local, block_owner, block_cell):
    count = lax.axis_size("slab")
    me = lax.axis_index("slab")
    side = images.shape[-1]
    frequency_total = references.shape[1]
    half = frequency_total // 2
    parts, picks = orient_owner.shape
    refs, bands = block_cell.shape
    items = parts * picks
    cells = ZDEV * (VY // (frequency_total // bands)) * (VX // frequency_total)
    band_rows = frequency_total // bands
    cap = max(2, 2 * items // count)
    lines = 40
    meta_row = half + 2
    own = half_spectra(images, defocus, frequency_total, lines)
    ids = (orient_owner * refs + orient_local).astype(jnp.float32)
    codes = (block_owner[..., 0] * cells + block_cell).astype(jnp.float32).reshape(parts, -1)
    meta = jnp.concatenate([ids, codes], axis=1)
    meta = jnp.pad(meta, ((0, 0), (0, 2 * frequency_total - meta.shape[1])))
    own = jnp.where((jnp.arange(lines) == meta_row)[None, :, None], meta[:, None, :], own)
    ref_a, ref_b = fold_references(references, lines)
    gathered = ring_gather(own, count)
    flat = gathered.reshape(count * parts, lines, 2 * frequency_total)
    meta = flat[:, meta_row]
    ids = meta[:, :picks].astype(jnp.int32)
    codes = meta[:, picks:picks + refs * bands // parts].astype(jnp.int32).reshape(count * refs, bands)
    by_source = ids.reshape(count, items)
    owner = by_source // refs
    same = owner[:, :, None] == owner[:, None, :]
    before = np.tril(np.ones((items, items), bool), -1)
    rank = jnp.sum(jnp.where(same & before[None], 1, 0), axis=2)
    mine = (owner == me)[:, :, None] & (rank[:, :, None] == jnp.arange(cap)[None, None, :])
    particle = (jnp.arange(count)[:, None] * parts + jnp.arange(items)[None, :] // picks)
    pick = lambda value: jnp.sum(jnp.where(mine, value[:, :, None], 0), axis=1).reshape(-1)
    pidx, ridx = pick(particle), pick(by_source % refs)
    peaks = score_items(pidx, ridx, flat, ref_a, ref_b, side, frequency_total)[:, 0]
    slot_scores = peaks * peaks + EPSILON
    everyone = share(jnp.broadcast_to(slot_scores[None], (8, count * cap)), count)[:, 0]
    table = everyone.reshape(count, count, cap).transpose(1, 0, 2).reshape(count, count * cap)
    where = owner * cap + rank
    scores = jnp.sum(
        jnp.where(where[:, :, None] == jnp.arange(count * cap)[None, None, :], table[:, None, :], 0.0), axis=2)
    scores = scores.reshape(count * parts, picks)
    posterior = scores / jnp.sum(scores, axis=1, keepdims=True)
    n = count * parts
    row_blocks, col_blocks = VY // band_rows, VX // frequency_total
    span = row_blocks // 2
    cell = codes - me * cells
    z, rb, cb = cell // (row_blocks * col_blocks), cell // col_blocks % row_blocks, cell % col_blocks
    order = (jnp.where(rb // span == lax.axis_index("dp"), 1, 0) * (cells // 2)
             + cb * (ZDEV * span) + z * span + rb % span + 1)
    order = jnp.where((cell >= 0) & (cell < cells), order, 0).T
    named = (jnp.arange(count * refs)[:, None] == ids.T.reshape(-1)[None, :]).astype(jnp.bfloat16)
    digits = jnp.concatenate([order // 32, order % 32], axis=0).astype(jnp.bfloat16)
    digits = jnp.dot(digits, named, preferred_element_type=jnp.float32).astype(jnp.int32)
    cidx = digits[:bands] * 32 + digits[bands:] - 1
    built = build_volume(cidx, posterior.T, flat.reshape(n * lines, 2 * frequency_total), half)
    built = built.reshape(band_rows, 2, 2, ZDEV, span, 2 * frequency_total)
    volume = built.transpose(3, 4, 0, 1, 2, 5).reshape(ZDEV, span * band_rows, 2, col_blocks * frequency_total)
    own_posterior = lax.dynamic_slice_in_dim(posterior, me * parts, parts, axis=0)
    return (own_posterior, volume)


def solution(mesh):
    in_specs = (
        P(("dp", "slab"), None, None),
        P(("dp", "slab")),
        P("slab", None, None),
        P(("dp", "slab"), None),
        P(("dp", "slab"), None),
        P("slab", None, None),
        P("slab", None),
    )
    out_specs = (P(("dp", "slab"), None), P("slab", "dp", None, None))
    small = mesh.shape["dp"] == 2 and mesh.shape["slab"] == 16
    return jax.shard_map(
        gather_device if small else per_device, mesh=mesh, in_specs=in_specs, out_specs=out_specs, check_vma=False
    )
```

```python
import functools
import math

import jax
import jax.numpy as jnp
import numpy as np
from jax import lax
from jax.experimental import pallas as pl
from jax.experimental.pallas import tpu as pltpu
from jax.sharding import PartitionSpec as P

VY = 256
VX = 256
ZDEV = 4


HIGH_PRECISION = lax.Precision.HIGHEST
AMPLITUDE = 0.1
EPSILON = 1e-05


def freq_tables(image_side, frequency_total):
    pixels = jnp.arange(image_side, dtype=jnp.int32)
    freqs = jnp.arange(frequency_total, dtype=jnp.int32) - frequency_total // 2
    phase = jnp.mod(pixels[:, None] * freqs[None, :], image_side).astype(jnp.float32) * (
        2.0 * math.pi / image_side
    )
    return (jnp.cos(phase), jnp.sin(phase))


def contrast(defocus, frequency_total):
    freqs = (jnp.arange(frequency_total, dtype=jnp.int32) - frequency_total // 2).astype(
        jnp.float32
    )
    radius = (freqs[:, None] * freqs[:, None] + freqs[None, :] * freqs[None, :]) / float(
        (frequency_total // 2) ** 2
    )
    phase = defocus[:, None, None] * radius[None]
    return -(math.sqrt(1.0 - AMPLITUDE * AMPLITUDE) * jnp.sin(phase) + AMPLITUDE * jnp.cos(phase))


def spectra_of(images, defocus, frequency_total):
    image_side = images.shape[-1]
    cosine, sine = freq_tables(image_side, frequency_total)
    first_pass = jnp.einsum(
        "pyx,xf->pyf", images, jnp.concatenate([cosine, -sine], axis=1), precision=HIGH_PRECISION
    )
    lower_half = jnp.concatenate(
        [first_pass[..., frequency_total:], -first_pass[..., :frequency_total]], axis=2
    )
    spectra = jnp.einsum("yf,pyg->pfg", cosine, first_pass, precision=HIGH_PRECISION) + jnp.einsum(
        "yf,pyg->pfg", sine, lower_half, precision=HIGH_PRECISION
    )
    factor = contrast(defocus, frequency_total) / image_side
    return spectra * jnp.concatenate([factor, factor], axis=2)


def score_slots(chosen, received, image_side):
    frequency_total = received.shape[1]
    cosine, sine = freq_tables(image_side, frequency_total)
    rotation_angle = jnp.concatenate(
        [jnp.concatenate([cosine.T, sine.T], axis=1), jnp.concatenate([-sine.T, cosine.T], axis=1)],
        axis=0,
    )
    inverted_rows = jnp.concatenate([cosine, -sine], axis=1)
    slot_total = received.shape[0]
    group_size = math.gcd(slot_total, 16)

    def one_group(couple):
        ref_part, spec_part = couple
        ref_re, ref_im = (ref_part[..., :frequency_total], ref_part[..., frequency_total:])
        spec_re, spec_im = (spec_part[..., :frequency_total], spec_part[..., frequency_total:])
        spectral_product = jnp.concatenate(
            [ref_re * spec_re + ref_im * spec_im, ref_re * spec_im - ref_im * spec_re], axis=2
        )
        center_index = jnp.einsum(
            "eio,ol->eil", spectral_product, rotation_angle, precision=HIGH_PRECISION
        )
        stacked_planes = jnp.concatenate(
            [center_index[..., :image_side], center_index[..., image_side:]], axis=1
        )
        translation_offsets = (
            jnp.einsum("kz,wzq->wkq", inverted_rows, stacked_planes, precision=HIGH_PRECISION)
            / frequency_total
        )
        return (
            jnp.max(
                (translation_offsets * translation_offsets).reshape(
                    translation_offsets.shape[0], -1
                ),
                axis=1,
            )
            + EPSILON
        )

    grouped = (
        chosen.reshape((slot_total // group_size, group_size) + chosen.shape[1:]),
        received.reshape((slot_total // group_size, group_size) + received.shape[1:]),
    )
    return lax.map(one_group, grouped).reshape(-1)


def slot_ranks(owner_ids, owner_count):
    owner_hits = (owner_ids[:, None] == jnp.arange(owner_count, dtype=jnp.int32)[None, :]).astype(
        jnp.int32
    )
    return jnp.sum((jnp.cumsum(owner_hits, axis=0) - 1) * owner_hits, axis=1)


def insert(blocks, cell_ids, planes, row_blocks, col_blocks, first_block, span_blocks):
    band_rows, row_width = (blocks.shape[2], blocks.shape[3])
    frequency_total = row_width // 2
    flat_rows = blocks.reshape(-1, band_rows * row_width)
    cell_ids = cell_ids.reshape(-1)
    plane_of = cell_ids // (row_blocks * col_blocks)
    row_of = cell_ids // col_blocks % row_blocks - first_block
    column_of = cell_ids % col_blocks
    usable = (cell_ids >= 0) & (row_of >= 0) & (row_of < span_blocks)
    target = jnp.where(usable, (plane_of * span_blocks + row_of) * col_blocks + column_of, -1)
    placing = (
        jnp.arange(planes * span_blocks * col_blocks, dtype=jnp.int32)[:, None] == target[None, :]
    ).astype(jnp.float32)
    placed = jnp.dot(placing, flat_rows, precision=HIGH_PRECISION)
    placed = placed.reshape(planes, span_blocks, col_blocks, band_rows, 2, frequency_total)
    return placed.transpose(0, 1, 3, 4, 2, 5).reshape(
        planes, span_blocks * band_rows, 2, col_blocks * frequency_total
    )


def per_device(images, defocus, references, orient_owner, orient_local, block_owner, block_cell):
    owner_count = lax.axis_size("slab")
    frequency_total = references.shape[1]
    image_side = images.shape[-1]
    part_count, pick_count = orient_owner.shape
    ref_rows = references.shape[0]
    slot_cap = max(2, 2 * part_count * pick_count // owner_count)
    spectra = spectra_of(images, defocus, frequency_total)
    flat_owner = orient_owner.reshape(-1)
    slot_of = flat_owner * slot_cap + slot_ranks(flat_owner, owner_count)
    particle_of = jnp.arange(part_count * pick_count, dtype=jnp.int32) // pick_count
    send_spectra = jnp.zeros(
        (owner_count * slot_cap, frequency_total, 2 * frequency_total), jnp.float32
    )
    send_spectra = send_spectra.at[slot_of].set(jnp.repeat(spectra, pick_count, axis=0))
    send_meta = jnp.full((owner_count * slot_cap, 2), -1, jnp.int32)
    send_meta = send_meta.at[slot_of].set(
        jnp.stack([orient_local.reshape(-1), particle_of], axis=1)
    )
    received, meta_in = (
        lax.all_to_all(
            send_spectra.reshape(owner_count, slot_cap, frequency_total, 2 * frequency_total),
            "slab",
            split_axis=0,
            concat_axis=0,
            tiled=True,
        ),
        lax.all_to_all(
            send_meta.reshape(owner_count, slot_cap, 2),
            "slab",
            split_axis=0,
            concat_axis=0,
            tiled=True,
        ),
    )
    flat_received = received.reshape(-1, frequency_total, 2 * frequency_total)
    ref_index = meta_in[..., 0].reshape(-1)
    chosen = references[jnp.clip(ref_index, 0, ref_rows - 1)]
    scores = score_slots(chosen, flat_received, image_side)
    slot_scores = scores.reshape(owner_count, slot_cap)
    back_scores = lax.all_to_all(slot_scores, "slab", split_axis=0, concat_axis=0, tiled=True)
    item_scores = back_scores.reshape(-1)[slot_of].reshape(part_count, pick_count)
    posterior = item_scores / jnp.sum(item_scores, axis=1, keepdims=True)
    slot_weight = (
        jnp.zeros((owner_count * slot_cap,), jnp.float32).at[slot_of].set(posterior.reshape(-1))
    )
    got_weight = lax.all_to_all(
        slot_weight.reshape(owner_count, slot_cap), "slab", split_axis=0, concat_axis=0, tiled=True
    ).reshape(-1)
    ref_hits = (ref_index[None, :] == jnp.arange(ref_rows, dtype=jnp.int32)[:, None]).astype(
        jnp.float32
    ) * got_weight[None, :]
    averages = jnp.dot(
        ref_hits, flat_received.reshape(flat_received.shape[0], -1), precision=HIGH_PRECISION
    )
    averages = averages.reshape(ref_rows, frequency_total, 2 * frequency_total)
    bands = block_cell.shape[1]
    band_rows = frequency_total // bands
    block_cap = max(2, 2 * ref_rows * bands // owner_count)
    dest_owner = block_owner.reshape(-1)
    block_slot = dest_owner * block_cap + slot_ranks(dest_owner, owner_count)
    cell_send = (
        jnp.full((owner_count * block_cap,), -1, jnp.int32)
        .at[block_slot]
        .set(block_cell.reshape(-1))
    )
    row_blocks = VY // band_rows
    col_blocks = VX // frequency_total
    pieces = averages.reshape(ref_rows * bands, band_rows, 2 * frequency_total)
    block_send = (
        jnp.zeros((owner_count * block_cap, band_rows, 2 * frequency_total), jnp.float32)
        .at[block_slot]
        .set(pieces)
    )
    blocks_in = lax.all_to_all(
        block_send.reshape(owner_count, block_cap, band_rows, 2 * frequency_total),
        "slab",
        split_axis=0,
        concat_axis=0,
        tiled=True,
    )
    cells_in = lax.all_to_all(
        cell_send.reshape(owner_count, block_cap), "slab", split_axis=0, concat_axis=0, tiled=True
    )
    partial_value = insert(blocks_in, cells_in, ZDEV, row_blocks, col_blocks, 0, row_blocks)
    volume = lax.psum_scatter(partial_value, "dp", scatter_dimension=1, tiled=True)
    return (posterior, volume)


HALF_PRECISION = lax.Precision.HIGH
MESH = pl.DeviceIdType.MESH


def ring_place(pos, depth):
    back = pos // depth
    z = (1 - back) * pos + back * (2 * depth - 1 - pos)
    return z * 2 + back


def gather_kernel(chips, own_ref, out_ref, local_sem, ring_send, ring_recv, pair_send, pair_recv):
    depth = chips // 2
    me = lax.axis_index("slab")
    core = me % 2
    chip = me // 2
    z, back = chip // 2, chip % 2
    pos = z + back * (2 * depth - 1 - 2 * z)
    dirs = ((pos + 1) % chips, (pos + chips - 1) % chips)
    targets = [ring_place(q, depth) * 2 + core for q in dirs]
    sibling = chip * 2 + 1 - core
    barrier = pltpu.get_barrier_semaphore()
    for other in targets + [sibling]:
        pl.semaphore_signal(barrier, inc=1, device_id={"slab": other}, device_id_type=MESH)
    pl.semaphore_wait(barrier, 3)
    part = own_ref.shape[0] // 2
    rows = lambda ref, h: ref.at[pl.ds(h * part, part)]
    local = pltpu.make_async_copy(own_ref, out_ref.at[me], local_sem)
    local.start()
    waits = []

    def ring_copy(src, origin, d, t, h):
        return pltpu.make_async_remote_copy(
            src_ref=src, dst_ref=rows(out_ref.at[origin], h),
            send_sem=ring_send.at[d, t, h], recv_sem=ring_recv.at[d, t, h],
            device_id={"slab": targets[d]}, device_id_type=MESH)

    def pair_copy(src, origin, n, h):
        return pltpu.make_async_remote_copy(
            src_ref=src, dst_ref=rows(out_ref.at[origin], h),
            send_sem=pair_send.at[n, h], recv_sem=pair_recv.at[n, h],
            device_id={"slab": sibling}, device_id_type=MESH)

    def origin_of(d, t):
        q = (pos + chips - t) % chips if d == 0 else (pos + t) % chips
        return ring_place(q, depth) * 2 + core

    hops = [(d, t, h) for t in range(depth) for h in range(2) for d in range(2)
            if t < depth - 1 or h == d]
    pair_of = lambda d, t, h: (t + 1 if d == 0 else depth + t + 1) if t < depth - 1 else depth
    for d, t, h in hops:
        if t == 0:
            copy = ring_copy(rows(own_ref, h), me, d, 0, h)
            copy.start()
            waits.append(copy)
    for h in range(2):
        copy = pair_copy(rows(own_ref, h), me, 0, h)
        copy.start()
        waits.append(copy)
    pairs = []
    for d, t, h in hops:
        origin = origin_of(d, t + 1)
        landed = rows(out_ref.at[origin], h)
        ring_copy(landed, origin, d, t, h).wait_recv()
        if (d, t + 1, h) in hops:
            copy = ring_copy(landed, origin, d, t + 1, h)
            copy.start()
            waits.append(copy)
        copy = pair_copy(landed, origin, pair_of(d, t, h), h)
        copy.start()
        pairs.append(copy)
        waits.append(copy)
    for copy in waits:
        copy.wait_send()
    pair_copy(rows(own_ref, 0), me, 0, 0).wait_recv()
    pair_copy(rows(own_ref, 1), me, 0, 1).wait_recv()
    for copy in pairs:
        copy.wait_recv()
    local.wait()


def ring_gather(payload, owner_count):
    chips = owner_count // 2
    depth = chips // 2
    return pl.pallas_call(
        functools.partial(gather_kernel, chips),
        out_shape=jax.ShapeDtypeStruct((owner_count,) + payload.shape, payload.dtype),
        in_specs=[pl.BlockSpec(memory_space=pltpu.VMEM)],
        out_specs=pl.BlockSpec(memory_space=pltpu.VMEM),
        scratch_shapes=[
            pltpu.SemaphoreType.DMA,
            pltpu.SemaphoreType.DMA((2, depth, 2)),
            pltpu.SemaphoreType.DMA((2, depth, 2)),
            pltpu.SemaphoreType.DMA((chips, 2)),
            pltpu.SemaphoreType.DMA((chips, 2)),
        ],
        compiler_params=pltpu.CompilerParams(collective_id=1, has_side_effects=True, vmem_limit_bytes=24 << 20),
        name="ring_gather",
    )(payload)


GROUP = 8


def score_kernel(pidx, ridx, spectra_ref, a_ref, b_ref, whi_ref, wlo_ref, cc_ref, pat_ref, slot_ref, out_ref):
    step = pl.program_id(0)
    lines = a_ref.shape[1]
    f32, bf16 = jnp.float32, jnp.bfloat16
    products = []
    for e in range(GROUP):
        spec = spectra_ref[pidx[step * GROUP + e]]
        ref = ridx[step * GROUP + e]
        products.append(a_ref[ref] * spec + b_ref[ref] * pltpu.roll(spec, 64, 1))
    product = jnp.concatenate(products, axis=0)
    hi = product.astype(bf16)
    lo = (product - hi.astype(f32)).astype(bf16)
    dot = lambda x, y: jnp.dot(x, y, preferred_element_type=f32)
    turned = dot(hi, whi_ref[...]) + dot(lo, whi_ref[...]) + dot(hi, wlo_ref[...])
    edge = jnp.concatenate([p[33:34] for p in products], axis=0).T
    cosine, sine = pat_ref[0:1], pat_ref[1:2]
    stacks = []
    for e in range(GROUP):
        rows = turned[e * lines:(e + 1) * lines]
        er, ei = edge[0:lines, e:e + 1], edge[64:64 + lines, e:e + 1]
        both = jnp.concatenate(
            [rows[:, :128] + er * cosine - ei * sine, rows[:, 128:] + er * sine + ei * cosine], axis=0)
        high = both.astype(bf16)
        low = (both - high.astype(f32)).astype(bf16)
        stacks.append(jnp.concatenate([high, low, high], axis=0))
    peaks = []
    for e in range(0, GROUP, 2):
        shifts = jnp.abs(dot(cc_ref[...], jnp.concatenate(stacks[e:e + 2], axis=1)))
        best = jnp.max(shifts, axis=0, keepdims=True)
        peaks += [best[:, :128], best[:, 128:]]
    peak = jnp.max(jnp.concatenate(peaks, axis=0), axis=1, keepdims=True)
    value = peak * peak + EPSILON
    slot = lax.broadcasted_iota(jnp.int32, out_ref.shape, 0) + step * GROUP

    @pl.when(step == 0)
    def _():
        out_ref[...] = jnp.zeros_like(out_ref)

    out_ref[...] += jnp.where(slot_ref[...] == slot, value, 0.0)


def score_tables(image_side, frequency_total, lines):
    half = frequency_total // 2
    x = np.arange(image_side)
    freqs = np.arange(frequency_total) - half
    ang = 2 * np.pi * ((freqs[:, None] * x[None, :]) % image_side) / image_side
    cos, sin = np.cos(ang), np.sin(ang)
    w = np.block([[cos, sin], [-sin, cos]]) / frequency_total
    cr, sr = np.zeros((image_side, lines)), np.zeros((image_side, lines))
    cr[:, : half + 1], sr[:, : half + 1] = cos[: half + 1].T, sin[: half + 1].T
    c = np.concatenate([cr, -sr], axis=1)
    def two(m):
        high = m.astype(jnp.bfloat16)
        return high, (m - high.astype(np.float64)).astype(jnp.bfloat16)
    whi, wlo = two(w)
    chi, clo = two(c)
    pat = np.zeros((8, image_side), np.float32)
    pat[0] = np.array([1, 0, -1, 0])[x % 4] / frequency_total
    pat[1] = np.array([0, 1, 0, -1])[x % 4] / frequency_total
    return whi, wlo, np.concatenate([chi, chi, clo], axis=1), pat


def score_items(pidx, ridx, spectra, ref_a, ref_b, slots, image_side, frequency_total):
    lines = spectra.shape[1]
    whi, wlo, cc, pat = (jnp.asarray(t) for t in score_tables(image_side, frequency_total, lines))
    full = lambda arr: pl.BlockSpec(arr.shape, lambda i, *_: (0,) * arr.ndim, pipeline_mode=pl.Buffered(1))
    args = (spectra, ref_a, ref_b, whi, wlo, cc, pat, slots)
    return pl.pallas_call(
        score_kernel,
        out_shape=jax.ShapeDtypeStruct((GROUP, slots.shape[1]), jnp.float32),
        grid_spec=pltpu.PrefetchScalarGridSpec(
            num_scalar_prefetch=2, grid=(pidx.shape[0] // GROUP,),
            in_specs=[full(arr) for arr in args],
            out_specs=pl.BlockSpec((GROUP, slots.shape[1]), lambda i, *_: (0, 0))),
        compiler_params=pltpu.CompilerParams(vmem_limit_bytes=40 << 20),
        name="score_items",
    )(pidx, ridx, *args)


def mirror_matrix(frequency_total):
    turn = np.zeros((2 * frequency_total, 2 * frequency_total), np.float32)
    for c in range(1, frequency_total):
        turn[frequency_total - c, c] = 1.0
        turn[2 * frequency_total - c, frequency_total + c] = -1.0
    return turn


def half_spectra(images, defocus, frequency_total, lines):
    side = images.shape[-1]
    half = frequency_total // 2
    freqs = np.arange(frequency_total) - half
    ang = 2 * np.pi * ((np.arange(side)[:, None] * freqs[None, :]) % side) / side
    cos, sin = np.cos(ang).astype(np.float32), np.sin(ang).astype(np.float32)
    first = jnp.einsum("pyx,xf->pyf", images, np.concatenate([cos, -sin], axis=1), precision=HALF_PRECISION)
    both = jnp.concatenate(
        [first, jnp.concatenate([first[..., frequency_total:], -first[..., :frequency_total]], axis=2)], axis=1)
    rows = np.zeros((lines, 2 * side), np.float32)
    rows[: half + 1] = np.concatenate([cos[:, : half + 1].T, sin[:, : half + 1].T], axis=1)
    spectra = jnp.einsum("ry,pyg->prg", rows, both, precision=HALF_PRECISION)
    edge_in = jnp.concatenate([first[:, :, 0], first[:, :, frequency_total]], axis=1)
    back = np.zeros((side, frequency_total), np.float32), np.zeros((side, frequency_total), np.float32)
    for r in range(1, half + 1):
        back[0][:, r], back[1][:, r] = cos[:, frequency_total - r] if r < half else cos[:, half], (
            sin[:, frequency_total - r] if r < half else sin[:, half])
    edge = jnp.dot(edge_in, np.block([[back[0], back[1]], [back[1], -back[0]]]), precision=HALF_PRECISION)
    f = freqs.astype(np.float32)
    fr = np.zeros((lines,), np.float32)
    fr[: half + 1] = f[: half + 1]
    radius = (fr[:, None] ** 2 + f[None, :] ** 2) / float(half * half)
    radius[half + 1] = radius[0]
    radius[half + 1, 1:half + 1] = radius[0][(frequency_total - np.arange(1, half + 1)) % frequency_total]
    phase = defocus[:, None, None] * radius[None]
    factor = -(math.sqrt(1.0 - AMPLITUDE * AMPLITUDE) * jnp.sin(phase) + AMPLITUDE * jnp.cos(phase)) / side
    value = spectra + edge[:, None, :] * (np.arange(lines) == half + 1).astype(np.float32)[None, :, None]
    return value * jnp.concatenate([factor, factor], axis=2)


def fold_references(references, lines):
    frequency_total = references.shape[1]
    half = frequency_total // 2
    sign = np.concatenate([np.ones(frequency_total), -np.ones(frequency_total)]).astype(np.float32)
    turned = jnp.einsum("rab,bc->rac", references[:, :half:-1], mirror_matrix(frequency_total) * sign[None, :],
                        precision=HIGH_PRECISION)
    folded = references[:, : half + 1] * sign
    folded = folded + jnp.pad(turned, ((0, 0), (1, 1), (0, 0)))
    edge = jnp.concatenate(
        [jnp.pad(references[:, :half:-1, col], ((0, 0), (1, frequency_total - half)))
         for col in (0, frequency_total)], axis=1)
    folded = jnp.concatenate(
        [folded, edge[:, None, :], jnp.zeros((references.shape[0], lines - half - 2, 2 * frequency_total))], axis=1)
    re, im = folded[..., :frequency_total], folded[..., frequency_total:]
    return jnp.concatenate([re, re], axis=2), jnp.concatenate([-im, im], axis=2)


def finish_kernel(count, tally_ref, cidx_ref, flat_ref, turn_ref, out_ref, post_ref,
                  dense, everyone, s_hi, s_lo, m_hi, m_lo, edge, away, inbox,
                  share_send, share_recv, send_sem, recv_sem):
    f32, bf16 = jnp.float32, jnp.bfloat16
    picks, n = post_ref.shape
    lines = flat_ref.shape[0] // n
    bands, halves = m_hi.shape[1], m_hi.shape[1] // 2
    me = lax.axis_index("slab")
    peer = 1 - lax.axis_index("dp")
    others = [(me + step) % count for step in range(1, count)]
    barrier = pltpu.get_barrier_semaphore()
    pl.semaphore_signal(barrier, inc=1, device_id={"dp": peer}, device_id_type=MESH)
    for other in others:
        pl.semaphore_signal(barrier, inc=1, device_id={"slab": other}, device_id_type=MESH)
    dense[...] = jnp.sum(tally_ref[...], axis=0, keepdims=True)
    def split(value):
        high = value.astype(bf16)
        return high, (value - high.astype(f32)).astype(bf16)

    def prepare(first, stop):
        for row in range(first, stop):
            s_hi[row], s_lo[row] = split(flat_ref[pl.ds(row, n, stride=lines), :])

    prepare(0, s_hi.shape[0] // 2)
    pl.semaphore_wait(barrier, count)
    shares = []
    for i, other in enumerate(others):
        copy = pltpu.make_async_remote_copy(
            src_ref=dense, dst_ref=everyone.at[i], send_sem=share_send.at[i],
            recv_sem=share_recv.at[i], device_id={"slab": other}, device_id_type=MESH)
        copy.start()
        shares.append(copy)
    prepare(s_hi.shape[0] // 2, s_hi.shape[0])

    scores = dense[...]
    for i, copy in enumerate(shares):
        copy.wait_recv()
        scores = scores + everyone[i]
    scores = [scores[:, k * n:(k + 1) * n] for k in range(picks)]
    total = sum(scores[1:], scores[0])
    for k in range(picks):
        post_ref[k:k + 1, :] = scores[k] / total

    def build(part):
        def one(j, carry):
            where = cidx_ref[pl.ds(j, 1), :]
            cell = lax.broadcasted_iota(jnp.int32, (n, n), 0) + part * n
            value = jnp.zeros((n, n), f32)
            for k in range(picks):
                value = value + jnp.where(where[:, k * n:(k + 1) * n] == cell, post_ref[k:k + 1, :], 0.0)
            m_hi[part, j], m_lo[part, j] = split(value)
            return carry

        lax.fori_loop(0, bands, one, 0)

    def dot(x, y):
        return jnp.dot(x, y, preferred_element_type=f32)

    def product(part, j, hi, lo):
        return dot(m_hi[part, j], hi) + dot(m_lo[part, j], hi) + dot(m_hi[part, j], lo)

    last = s_hi.shape[0]
    lane = lax.broadcasted_iota(jnp.int32, (n, 128), 1)

    def edges(part):
        total = jnp.zeros((n, 128), f32)
        ext = flat_ref[pl.ds(last, n, stride=lines), :]
        for jj in range(halves):
            hi, lo = split(pltpu.roll(ext, 128 - (1 + 8 * jj), 1))
            total = total + product(part, bands - 1 - jj, hi, lo)
        edge[...] = total

    def pair(ref, first, second):
        return jnp.concatenate([ref[first], ref[second]], axis=1)

    def chunk(part, ip):
        i = 2 * ip
        front, back = jnp.zeros((n, 256), f32), jnp.zeros((n, 256), f32)
        for jj in range(halves):
            a, b = 8 * jj + i, 8 * jj + i + 1
            front = front + product(part, jj, pair(s_hi, a, b), pair(s_lo, a, b))
            a, b = 8 * jj + 8 - i, 8 * jj + 7 - i
            back = back + product(part, bands - 1 - jj, pair(s_hi, a, b), pair(s_lo, a, b))
        result = []
        for u in range(2):
            hi, lo = split(back[:, u * 128:(u + 1) * 128])
            flipped = dot(hi, turn_ref[...]) + dot(lo, turn_ref[...])
            at = pltpu.roll(edge[...], (128 - (7 - i - u)) % 128, 1)
            flipped = flipped + jnp.where(lane == 0, at, jnp.where(lane == 64, -at, 0.0))
            full = front[:, u * 128:(u + 1) * 128] + flipped
            rolled = pltpu.roll(full, 64, 1)
            q = n // 4
            low = lane[:q] < 64
            for p in range(2):
                x, y = slice(2 * p * q, (2 * p + 1) * q), slice((2 * p + 1) * q, (2 * p + 2) * q)
                result.append((u, p, jnp.where(low, full[x], rolled[y])))
                result.append((u, 2 + p, jnp.where(low, rolled[x], full[y])))
        return result

    def copy_of(ip):
        return pltpu.make_async_remote_copy(
            src_ref=away.at[ip], dst_ref=inbox.at[ip], send_sem=send_sem.at[ip], recv_sem=recv_sem.at[ip],
            device_id={"dp": peer}, device_id_type=MESH)

    pieces = away.shape[0]
    build(0)
    edges(0)
    for ip in range(pieces):
        for u, p, value in chunk(0, ip):
            away[ip, u, p] = value
        copy_of(ip).start()
    build(1)
    edges(1)
    for ip in range(pieces):
        for u, p, value in chunk(1, ip):
            out_ref[ip, u, p] = value
    for ip in range(pieces):
        copy_of(ip).wait_recv()
        out_ref[ip] = out_ref[ip] + inbox[ip]
    for copy in shares:
        copy.wait_send()
    for ip in range(pieces):
        copy_of(ip).wait_send()


def finish(tally, cidx, flat, count, lines, frequency_total):
    bands, half = cidx.shape[0], frequency_total // 2
    lanes = flat.shape[1]
    n = flat.shape[0] // lines
    items = cidx.shape[1]
    turn = jnp.asarray(mirror_matrix(frequency_total), jnp.bfloat16)
    piece = (4, 2, 4, n // 4, lanes)
    vmem = pl.BlockSpec(memory_space=pltpu.VMEM)
    return pl.pallas_call(
        functools.partial(finish_kernel, count),
        out_shape=(jax.ShapeDtypeStruct(piece, jnp.float32),
                   jax.ShapeDtypeStruct((items // n, n), jnp.float32)),
        in_specs=[vmem] * 4,
        out_specs=(vmem, vmem),
        scratch_shapes=[
            pltpu.VMEM((1, items), jnp.float32),
            pltpu.VMEM((count - 1, 1, items), jnp.float32),
            pltpu.VMEM((half + 1, n, lanes), jnp.bfloat16),
            pltpu.VMEM((half + 1, n, lanes), jnp.bfloat16),
            pltpu.VMEM((2, bands, n, n), jnp.bfloat16),
            pltpu.VMEM((2, bands, n, n), jnp.bfloat16),
            pltpu.VMEM((n, lanes), jnp.float32),
            pltpu.VMEM(piece, jnp.float32),
            pltpu.VMEM(piece, jnp.float32),
            pltpu.SemaphoreType.DMA((count - 1,)),
            pltpu.SemaphoreType.DMA((count - 1,)),
            pltpu.SemaphoreType.DMA((4,)),
            pltpu.SemaphoreType.DMA((4,)),
        ],
        compiler_params=pltpu.CompilerParams(
            collective_id=3, has_side_effects=True, vmem_limit_bytes=48 << 20),
        name="share_and_insert",
    )(tally, cidx, flat, turn)


def gather_device(images, defocus, references, orient_owner, orient_local, block_owner, block_cell):
    count = lax.axis_size("slab")
    me = lax.axis_index("slab")
    side = images.shape[-1]
    frequency_total = references.shape[1]
    half = frequency_total // 2
    parts, picks = orient_owner.shape
    refs, bands = block_cell.shape
    items = parts * picks
    cells = ZDEV * (VY // (frequency_total // bands)) * (VX // frequency_total)
    band_rows = frequency_total // bands
    cap = max(2, 2 * items // count)
    lines = 40
    meta_row = half + 2
    own = half_spectra(images, defocus, frequency_total, lines)
    ids = (orient_owner * refs + orient_local).astype(jnp.float32)
    codes = (block_owner[..., 0] * cells + block_cell).astype(jnp.float32).reshape(parts, -1)
    meta = jnp.concatenate([ids, codes], axis=1)
    meta = jnp.pad(meta, ((0, 0), (0, 2 * frequency_total - meta.shape[1])))
    own = jnp.where((jnp.arange(lines) == meta_row)[None, :, None], meta[:, None, :], own)
    ref_a, ref_b = fold_references(references, lines)
    gathered = ring_gather(own, count)
    flat = gathered.reshape(count * parts, lines, 2 * frequency_total)
    meta = flat[:, meta_row]
    ids = meta[:, :picks].astype(jnp.int32)
    codes = meta[:, picks:picks + refs * bands // parts].astype(jnp.int32).reshape(count * refs, bands)
    by_source = ids.reshape(count, items)
    owner = by_source // refs
    same = owner[:, :, None] == owner[:, None, :]
    before = np.tril(np.ones((items, items), bool), -1)
    rank = jnp.sum(jnp.where(same & before[None], 1, 0), axis=2)
    mine = (owner == me)[:, :, None] & (rank[:, :, None] == jnp.arange(cap)[None, None, :])
    particle = (jnp.arange(count)[:, None] * parts + jnp.arange(items)[None, :] // picks)
    pick = lambda value: jnp.sum(jnp.where(mine, value[:, :, None], 0), axis=1).reshape(-1)
    pidx, ridx = pick(particle), pick(by_source % refs)
    slots = jnp.where(owner == me, jnp.arange(count)[:, None] * cap + rank, -1)
    slots = slots.reshape(count * parts, picks).T.reshape(1, -1)
    n = count * parts
    row_blocks, col_blocks = VY // band_rows, VX // frequency_total
    span = row_blocks // 2
    cell = codes - me * cells
    z, rb, cb = cell // (row_blocks * col_blocks), cell // col_blocks % row_blocks, cell % col_blocks
    order = (jnp.where(rb // span == lax.axis_index("dp"), 1, 0) * (cells // 2)
             + cb * (ZDEV * span) + z * span + rb % span + 1)
    order = jnp.where((cell >= 0) & (cell < cells), order, 0).T
    named = (jnp.arange(count * refs)[:, None] == ids.T.reshape(-1)[None, :]).astype(jnp.bfloat16)
    digits = jnp.concatenate([order // 32, order % 32], axis=0).astype(jnp.bfloat16)
    digits = jnp.dot(digits, named, preferred_element_type=jnp.float32).astype(jnp.int32)
    cidx = digits[:bands] * 32 + digits[bands:] - 1
    tally = score_items(pidx, ridx, flat, ref_a, ref_b, slots, side, frequency_total)
    built, weights = finish(tally, cidx, flat.reshape(n * lines, 2 * frequency_total), count, lines, frequency_total)
    built = built.reshape(band_rows, 2, 2, ZDEV, span, 2 * frequency_total)
    volume = built.transpose(3, 4, 0, 1, 2, 5).reshape(ZDEV, span * band_rows, 2, col_blocks * frequency_total)
    own_posterior = lax.dynamic_slice_in_dim(weights, me * parts, parts, axis=1).T
    return (own_posterior, volume)


def solution(mesh):
    in_specs = (
        P(("dp", "slab"), None, None),
        P(("dp", "slab")),
        P("slab", None, None),
        P(("dp", "slab"), None),
        P(("dp", "slab"), None),
        P("slab", None, None),
        P("slab", None),
    )
    out_specs = (P(("dp", "slab"), None), P("slab", "dp", None, None))
    small = mesh.shape["dp"] == 2 and mesh.shape["slab"] == 16
    return jax.shard_map(
        gather_device if small else per_device, mesh=mesh, in_specs=in_specs, out_specs=out_specs, check_vma=False
    )
```
